128 devices in a mesh: facet: 16 (over x, y), sub: 8 (over z, core).
Axes of the slice: x: 4, y: 4, z: 4, core: 2. Of those that a mesh axis runs over, the one named last changes fastest.
Arguments:
- strips: bfloat16 [16, 64, 8192], P('facet', 'sub'), may hold values from -6 to 6
- facet_offset: int32 [16], replicated, may hold values from 0 to 448
- subgrid_offset: int32 [128], replicated, may hold values from 0 to 4095
- owner: int32 [128], replicated, may hold values from 0 to 127, as said below
- screen_index: int32 [128], replicated, may hold values from 0 to 15
- screens: bfloat16 [16, 64, 1024], replicated, may hold values from -1 to 1, as said below
- grid_weight: float32 [512, 512], P(('facet', 'sub')), may hold values from 0.3 to 3
Outputs:
- facet_out: float32 [16, 64, 8192], P('facet', 'sub')
The draws below stay inside these ranges and needn't reach their ends.
Inputs may be any that keep to these rules, and one draw needn't show every extreme that they name: `owner`: device number i * 8 + k is the device at index i of facet and k of sub. No device owns more than 4 subgrids, and some device owns exactly 4. `screens`: element g and element 512 + g of a row are the cosine and sine of one phase.
All inputs are finite; a program needn't handle non-finite values.
Results may differ from the reference program's by a relative error of at most 0.0059.
Values may be sent and summed in bfloat16 or wider, within the bound.
A program may use at most 64 MiB of HBM per device.

```python
import math
import jax
import jax.numpy as jnp
from jax import lax

FL = 4096
M = 64
SG = 512
WS = 16
CAP = 4
FACETS = 16
COLS = 64
OWNERS = 128
SUBGRIDS = 128


def draw_owner(key, part):
    first_key = jax.random.fold_in(key, 11)
    second_key = jax.random.fold_in(key, 12)
    third_key = jax.random.fold_in(key, 13)
    slot_total = OWNERS * CAP
    slot_ids = jnp.arange(slot_total, dtype=jnp.int32)
    scores = jax.random.permutation(first_key, slot_total).astype(jnp.int32)
    busiest = jax.random.randint(second_key, (), 0, OWNERS, dtype=jnp.int32)
    scores = jnp.where(slot_ids // CAP == busiest, -CAP + slot_ids % CAP, scores)
    chosen = jnp.argsort(scores, stable=True)[:SUBGRIDS].astype(jnp.int32)
    owners_list = chosen // CAP
    return jax.random.permutation(third_key, owners_list).astype(jnp.int32)


def draw_screens(key, part):
    phase_key = jax.random.fold_in(key, 21)
    angles = jax.random.uniform(phase_key, (WS, COLS, SG), jnp.float32, -math.pi, math.pi)
    return jnp.concatenate([jnp.cos(angles), jnp.sin(angles)], axis=-1).astype(jnp.bfloat16)


def plant(drawn, rng, least, top_value):
    longest = drawn.shape.index(max(drawn.shape))
    spots = []
    for shift in (0, 1):
        where = [jax.random.randint(jax.random.fold_in(rng, axis), (), 0, length) for axis, length in enumerate(drawn.shape)]
        where[longest] = (where[longest] + shift) % drawn.shape[longest]
        spots.append(tuple(where))
    return drawn.at[spots[0]].set(least).at[spots[1]].set(top_value)


def steps_of(stream_key, shape, cuts, low, largest):
    def one(dim, shards_of):
        heights = jax.random.uniform(jax.random.fold_in(jax.random.fold_in(stream_key, 6), dim), (shards_of,), jnp.float32, low / len(cuts), largest / len(cuts))
        return jnp.repeat(jnp.exp(heights), shape[dim] // shards_of).reshape((-1,) + (1,) * (len(shape) - dim - 1))

    gain = one(*cuts[0])
    for cut in cuts[1:]:
        gain = gain * one(*cut)
    return gain


def centred(rng, shape, deviation, limit, cuts=(), kind=jnp.bfloat16):
    entries = deviation * jax.random.normal(rng, shape, jnp.float32)
    if cuts:
        entries = entries * steps_of(rng, shape, cuts, -0.22, 0.18)
    return jnp.clip(entries, -limit, limit).astype(kind)


def setup_inputs(seed: int = 0) -> dict:
    splits = jax.random.split(jax.random.key(seed), 8)
    return {
        "strips": centred(splits[0], (FACETS, COLS, 2 * FL), 1.0, 6.0, ((0, 16), (1, 8))),
        "facet_offset": plant(jax.random.randint(splits[1], (FACETS,), 0, SG - M + 1), jax.random.fold_in(splits[1], 1), 0, SG - M).astype(jnp.int32),
        "subgrid_offset": plant(jax.random.randint(splits[2], (SUBGRIDS,), 0, FL), jax.random.fold_in(splits[2], 1), 0, FL - 1).astype(jnp.int32),
        "owner": draw_owner(jax.random.fold_in(splits[7], 71), 0),
        "screen_index": plant(jax.random.randint(splits[4], (SUBGRIDS,), 0, WS), jax.random.fold_in(splits[4], 1), 0, WS - 1).astype(jnp.int32),
        "screens": draw_screens(jax.random.fold_in(splits[7], 71), 0),
        "grid_weight": jnp.clip(jnp.exp(math.log(3.0) - 2.3025851 * jax.random.uniform(splits[6], (OWNERS * CAP, SG), jnp.float32) ** steps_of(splits[6], (OWNERS * CAP, SG), ((0, 128),), -0.2, 0.2)), 0.3, 3.0),
    }


def table_block(start, length, count):
    points = jnp.arange(length, dtype=jnp.int32)
    orders = start + jnp.arange(count, dtype=jnp.int32)
    turn_counts = points[:, None] * orders[None, :] % length
    angles = turn_counts.astype(jnp.float32) * (2.0 * math.pi / length)
    factor = 1.0 / math.sqrt(length)
    cosine = jnp.cos(angles) * factor
    sine_part = jnp.sin(angles) * factor
    upper = jnp.concatenate([cosine, -sine_part], axis=1)
    lower = jnp.concatenate([sine_part, cosine], axis=1)
    return jnp.concatenate([upper, lower], axis=0).astype(jnp.bfloat16)

def full_spectrum(rows):
    width = min(FL, 512)
    blocks = FL // width
    row_count = rows.shape[0]

    def one_block(index):
        block = table_block(index * width, FL, width)
        product = jnp.dot(rows, block, preferred_element_type=jnp.float32)
        return product.astype(jnp.bfloat16).reshape(row_count, 2, width)
    pieces = lax.map(one_block, jnp.arange(blocks, dtype=jnp.int32))
    return jnp.transpose(pieces, (1, 2, 0, 3)).reshape(row_count, 2 * FL)

def synthesize(spectrum):
    width = min(FL, 512)
    blocks = FL // width
    row_count = spectrum.shape[0]
    shaped = spectrum.reshape(row_count, 2, blocks, width)

    def add_block(index, accumulated):
        block = table_block(index * width, FL, width)
        piece = lax.dynamic_index_in_dim(shaped, index, 2, keepdims=False).reshape(row_count, 2 * width)
        return accumulated + lax.dot_general(piece, block, (((1,), (1,)), ((), ())), preferred_element_type=jnp.float32)
    return lax.fori_loop(jnp.int32(0), jnp.int32(blocks), add_block, jnp.zeros((row_count, 2 * FL), jnp.float32))

def reference(strips, facet_offset, subgrid_offset, owner, screen_index, screens, grid_weight):
    subgrid_ids = jnp.arange(SUBGRIDS, dtype=jnp.int32)
    orders = jnp.arange(M, dtype=jnp.int32)
    spectrum = full_spectrum(strips.reshape(FACETS * COLS, 2 * FL)).reshape(FACETS, COLS, 2 * FL)
    frequencies = (subgrid_offset[None, :, None] + facet_offset[:, None, None] + orders[None, None, :]) % FL

    def facet_forward(facet_number):
        spec_f = spectrum[facet_number]
        chosen = frequencies[facet_number]
        real_part = jnp.transpose(spec_f[:, chosen], (1, 0, 2))
        imag_part = jnp.transpose(spec_f[:, FL + chosen], (1, 0, 2))
        return jnp.concatenate([real_part, imag_part], axis=2)
    contributions = lax.map(facet_forward, jnp.arange(FACETS, dtype=jnp.int32))
    onehot = (owner[:, None] == jnp.arange(OWNERS, dtype=jnp.int32)[None, :]).astype(jnp.int32)
    before = jnp.cumsum(onehot, axis=0) - onehot
    slot = lax.optimization_barrier(jnp.sum(before * onehot, axis=1))
    weight_row = owner * CAP + slot

    def process(subgrid):
        subgrid_sum = jnp.zeros((COLS, 2, SG), jnp.float32)
        starts = []
        for facet_number in range(FACETS):
            start = (jnp.int32(0), jnp.int32(0), facet_offset[facet_number].astype(jnp.int32))
            starts.append(start)
            piece = contributions[facet_number, subgrid].reshape(COLS, 2, M).astype(jnp.float32)
            current = lax.dynamic_slice(subgrid_sum, start, (COLS, 2, M))
            subgrid_sum = lax.dynamic_update_slice(subgrid_sum, current + piece, start)
        screen_f = screens[screen_index[subgrid]].reshape(COLS, 2, SG).astype(jnp.float32)
        weighting = grid_weight[weight_row[subgrid]][None, :]
        real_part = (subgrid_sum[:, 0] * screen_f[:, 0] - subgrid_sum[:, 1] * screen_f[:, 1]) * weighting
        imag_part = (subgrid_sum[:, 0] * screen_f[:, 1] + subgrid_sum[:, 1] * screen_f[:, 0]) * weighting
        processed = jnp.stack([real_part, imag_part], axis=1).astype(jnp.bfloat16)
        extracted = [lax.dynamic_slice(processed, start, (COLS, 2, M)).reshape(COLS, 2 * M) for start in starts]
        return jnp.stack(extracted, axis=0)
    returned = lax.map(process, subgrid_ids)

    def facet_backward(facet_number):
        chosen = frequencies[facet_number]
        rows_f = jnp.transpose(returned[:, facet_number].astype(jnp.float32), (1, 0, 2))
        back = jnp.zeros((COLS, 2, FL), jnp.float32)
        back = back.at[:, 0, chosen].add(rows_f[:, :, :M])
        back = back.at[:, 1, chosen].add(rows_f[:, :, M:])
        return synthesize(back.reshape(COLS, 2 * FL).astype(jnp.bfloat16))
    return lax.map(facet_backward, jnp.arange(FACETS, dtype=jnp.int32))
```

```python
import functools
import math

import jax
import jax.numpy as jnp
import numpy as np
from jax import lax
from jax.experimental import pallas as pl
from jax.experimental.pallas import tpu as pltpu
from jax.sharding import PartitionSpec as P

FL = 4096
CAP = 4
NF = 16
NS = 8
ROWS = 8
MINE = 8
BLOCKS = 9
MESH = pl.DeviceIdType.MESH
F32 = jnp.float32
BF16 = jnp.bfloat16


def split_halves(table):
    high = table.astype(np.float32).astype(jnp.bfloat16)
    low = (table - high.astype(np.float64)).astype(np.float32).astype(jnp.bfloat16)
    return high, low


def make_tables():
    k = np.arange(64)
    u = np.arange(32)
    b = np.arange(128)
    tau = 2.0 * np.pi
    first = tau * ((2 * k[:, None] * u[None, :]) % 64) / 64
    twist = tau * ((k[:, None] * b[None, :]) % FL) / FL
    last = tau * ((k[:, None] * b[None, :]) % 64) / 64
    scale = 1.0 / math.sqrt(FL)
    c, s = np.cos(first) * scale, np.sin(first) * scale
    ahead = np.block([[c, s], [-s, c]])
    back = np.block([[c.T, -s.T], [s.T, c.T]])
    forward_rows = np.zeros((128, 256))
    forward_rows[:64, :128] = np.cos(last)
    forward_rows[:64, 128:] = np.sin(last)
    backward_rows = np.zeros((128, 128))
    backward_rows[:64, :64] = np.cos(last[:, :64]).T
    backward_rows[64:, :64] = np.sin(last[:, :64]).T
    ct, st = np.cos(twist), np.sin(twist)
    twist_ahead = np.stack([ct, st]).astype(np.float32)
    twist_back = np.stack([np.concatenate([ct.T, ct.T], 1), np.concatenate([-st.T, st.T], 1)]).astype(np.float32)
    return (
        np.stack(split_halves(ahead)),
        twist_ahead,
        np.stack(split_halves(forward_rows)),
        np.stack(split_halves(backward_rows)),
        twist_back,
        np.stack(split_halves(back)),
    )


def mm(a, b):
    return jnp.dot(a, b, preferred_element_type=F32)


def mm_nt(a, b):
    return lax.dot_general(a, b, (((1,), (1,)), ((), ())), preferred_element_type=F32)


def halves(x):
    high = x.astype(BF16)
    return high, (x - high.astype(F32)).astype(BF16)


def iota(shape, dim):
    return lax.broadcasted_iota(jnp.int32, shape, dim)


def kernel(
    fo, so, si, so_v, ow_v, strips, gw, ahead, twa, frow, brow, twb, back, screens, out,
    xs, col, qsc, wblk, bsc, scr, sbuf, rbuf, esend, ebuf, wmsg, wrows, wpart, wall, oscr,
    scr_sem, s1, r1, s2, r2, sw1, rw1, sw2, rw2,
):
    f = lax.axis_index("facet")
    s = lax.axis_index("sub")
    fx, fy = f // 4, f % 4
    steps = [(dx, dy) for dx in range(4) for dy in range(4) if (dx, dy) != (0, 0)]
    steps.sort(key=lambda d: -(min(d[0], 4 - d[0]) + min(d[1], 4 - d[1])))
    peers = [((fx + dx) % 4) * 4 + (fy + dy) % 4 for dx, dy in steps]
    senders = [((fx - dx + 4) % 4) * 4 + (fy - dy + 4) % 4 for dx, dy in steps]

    barrier = pltpu.get_barrier_semaphore()
    for p in peers:
        pl.semaphore_signal(barrier, inc=1, device_id=(p, s), device_id_type=MESH)
    for d in range(1, NS):
        pl.semaphore_signal(barrier, inc=1, device_id=(f, (s + d) % NS), device_id_type=MESH)

    screen_copy = pltpu.make_async_copy(screens.at[:, pl.ds(pl.multiple_of(s * ROWS, ROWS), ROWS), :], scr, scr_sem)
    screen_copy.start()

    for q in range(4):
        wmsg[pl.ds(4 * q, 4), :] = gw[:, 128 * q : 128 * q + 128]
    wrows[pl.ds(f, 1)] = wmsg[...].astype(BF16)[None]

    lane = iota((128, 128), 1)
    sub_i = iota((128, 128), 0)
    low6 = lane & 63
    so_row = jnp.broadcast_to(so_v[...], (128, 128))
    ow_row = jnp.broadcast_to(ow_v[...], (128, 128))
    so_col = jnp.transpose(so_row)
    ow_col = jnp.transpose(ow_row)
    earlier = jnp.where((ow_row == ow_col) & (lane < sub_i), 1.0, 0.0)
    slot = jnp.sum(earlier, axis=1, keepdims=True).astype(jnp.int32)
    col[0] = so_col
    col[1] = ow_col * CAP + slot

    my_offset = fo[f]
    start_col = (so_col + my_offset) & (FL - 1)
    q_col = start_col >> 6
    take_low = low6 >= (start_col & 63)
    start_row = (so_row + my_offset) & (FL - 1)
    q_row = start_row >> 6

    pick = jnp.concatenate(
        [jnp.where(lane == q_col, 1.0, 0.0), jnp.where(lane == ((q_col + 1) & 63), 1.0, 0.0)], axis=0
    ).astype(BF16)
    tf_high = mm(pick, frow[0]).astype(BF16)
    tf_low = mm(pick, frow[1]).astype(BF16)
    for v in range(64):
        xs[pl.ds(8 * v, 8), :] = strips[:, 128 * v : 128 * v + 128].astype(F32)
    tc, ts = twa[0], twa[1]

    def contributions(row):
        x = xs[pl.ds(row, 64, stride=8), :].astype(BF16)
        a = mm(ahead[0], x) + mm(ahead[1], x)
        re, im = a[:64], a[64:]
        b_re = re * tc + im * ts
        b_im = im * tc - re * ts
        b = jnp.concatenate(
            [jnp.concatenate([b_re, b_im], axis=1), jnp.concatenate([b_im, -b_re], axis=1)], axis=0
        )
        b_high, b_low = halves(b)
        g = mm_nt(tf_high, b_high) + mm_nt(tf_low, b_high) + mm_nt(tf_high, b_low)
        return jnp.where(take_low, g[:128], g[128:])

    for pair in range(ROWS // 2):
        c0 = contributions(2 * pair).reshape(NF, MINE, 128)
        c1 = contributions(2 * pair + 1).reshape(NF, MINE, 128)
        both = jnp.concatenate([c0, c1], axis=1).astype(BF16)
        sbuf[:, pair] = both
    rbuf[pl.ds(f, 1)] = sbuf[pl.ds(f, 1)]

    pl.semaphore_wait(barrier, NF - 1 + NS - 1)

    def remote(src, dst, send, recv, to):
        return pltpu.make_async_remote_copy(
            src_ref=src, dst_ref=dst, send_sem=send, recv_sem=recv, device_id=to, device_id_type=MESH
        )

    w1 = [remote(wrows.at[f], wrows.at[f], sw1.at[n], rw1.at[n], (p, s)) for n, p in enumerate(peers)]
    a1 = [remote(sbuf.at[p], rbuf.at[f], s1.at[n], r1.at[n], (p, s)) for n, p in enumerate(peers)]
    for c in w1:
        c.start()
    for c in a1:
        c.start()

    pick_t = jnp.concatenate(
        [jnp.where(sub_i == q_row, 1.0, 0.0), jnp.where(sub_i == ((q_row + 1) & 63), 1.0, 0.0)], axis=1
    ).astype(BF16)
    tb_high = mm(brow[0], pick_t).astype(BF16)
    tb_low = mm(brow[1], pick_t).astype(BF16)

    lane8 = iota((8, 128), 1)
    left = lane8 < 64
    base = pl.multiple_of(f * MINE, MINE)
    so8 = col[0, pl.ds(base, MINE), :]
    wr8 = col[1, pl.ds(base, MINE), :]
    r8 = so8 & 63
    zero = jnp.zeros((8, 128), F32)
    screen_copy.wait()

    def to_blocks(pieces):
        blocks = []
        for piece in pieces:
            other = pltpu.roll(piece, 64, 1)
            blocks.append(jnp.where(left, piece, other))
            blocks.append(jnp.where(left, other, piece))
        return blocks[:BLOCKS]

    for j in range(MINE):
        shift = so[base + j] & 63
        screen = scr[si[base + j]].astype(F32)
        for part in range(2):
            rolled = [
                pltpu.roll(screen[:, 512 * part + 128 * v : 512 * part + 128 * v + 128], shift, 1) for v in range(4)
            ]
            rolled = [zero] + rolled + [zero]
            pieces = [jnp.where(lane8 >= shift, rolled[v + 1], rolled[v]) for v in range(5)]
            for n, block in enumerate(to_blocks(pieces)):
                value = jnp.where(left, -block, block) if part else block
                qsc[part, n, pl.ds(j, ROWS, stride=MINE), :] = value

    for n in range(NF):
        start = r8 + fo[n]
        bsc[n] = (start >> 6) + jnp.where((lane8 & 63) < (start & 63), 1, 0)

    for n, p in enumerate(senders):
        remote(wrows.at[f], wrows.at[p], sw1.at[n], rw1.at[n], (p, s)).wait_recv()
    lane256 = iota((8, 256), 1)
    target = (lane256 >> 4) * (NS * CAP) + s * CAP + (lane256 & 3)
    wanted = jnp.concatenate([wr8, wr8], axis=1) == target
    chosen = jnp.concatenate(
        [jnp.where(wanted & (((lane256 >> 2) & 3) == q), 1.0, 0.0) for q in range(4)], axis=0
    ).astype(BF16)
    part_rows = mm(chosen, wrows[...].reshape(256, 128)).astype(BF16)
    wpart[...] = part_rows
    wall[pl.ds(s, 1)] = part_rows[None]
    w2 = [
        remote(wpart, wall.at[s], sw2.at[d - 1], rw2.at[d - 1], (f, (s + d) % NS)) for d in range(1, NS)
    ]
    for c in w2:
        c.start()
    for d in range(1, NS):
        p = (s - d + NS) % NS
        remote(wpart, wall.at[p], sw2.at[d - 1], rw2.at[d - 1], (f, p)).wait_recv()
    w32 = wall[0].astype(F32)
    for p in range(1, NS):
        w32 = w32 + wall[p].astype(F32)
    pieces = [w32[8 * q : 8 * q + 8] for q in range(4)] + [zero]
    for bit in range(6):
        amount = 1 << bit
        turned = [zero] + [pltpu.roll(piece, amount, 1) for piece in pieces]
        moved = [jnp.where(lane8 >= amount, turned[v + 1], turned[v]) for v in range(5)]
        on = (r8 & amount) != 0
        pieces = [jnp.where(on, moved[v], pieces[v]) for v in range(5)]
    for n, block in enumerate(to_blocks(pieces)):
        wblk[n] = block

    for n, p in enumerate(senders):
        remote(sbuf.at[p], rbuf.at[p], s1.at[n], r1.at[n], (p, s)).wait_recv()

    def process(pair, carry):
        got = [rbuf[n, pair].astype(F32) for n in range(NF)]
        sent = []
        for half in range(2):
            row = 2 * pair + half
            sums = [zero] * BLOCKS
            for n in range(NF):
                piece = got[n][8 * half : 8 * half + 8]
                where = bsc[n]
                for b in range(BLOCKS):
                    sums[b] = sums[b] + jnp.where(where == b, piece, 0.0)
            done = []
            at = pl.ds(pl.multiple_of(row * MINE, MINE), MINE)
            for b in range(BLOCKS):
                turned = pltpu.roll(sums[b], 64, 1)
                done.append((sums[b] * qsc[0, b, at, :] + turned * qsc[1, b, at, :]) * wblk[b])
            picked = []
            for n in range(NF):
                where = bsc[n]
                piece = done[0]
                for b in range(1, BLOCKS):
                    piece = jnp.where(where == b, done[b], piece)
                picked.append(piece)
            sent.append(picked)
        for n in range(NF):
            esend[n, pair] = jnp.concatenate([sent[0][n], sent[1][n]], axis=0).astype(BF16)
        return carry

    lax.fori_loop(0, ROWS // 2, process, 0)

    ebuf[pl.ds(f, 1)] = esend[pl.ds(f, 1)]
    a2 = [remote(esend.at[p], ebuf.at[f], s2.at[n], r2.at[n], (p, s)) for n, p in enumerate(peers)]
    for c in a2:
        c.start()
    for c in w1 + a1 + w2:
        c.wait_send()
    for n, p in enumerate(senders):
        remote(esend.at[p], ebuf.at[p], s2.at[n], r2.at[n], (p, s)).wait_recv()

    bc, bs = twb[0], twb[1]
    sign = jnp.where(iota((64, 128), 1) < 64, -1.0, 1.0)
    for row in range(ROWS):
        e = ebuf[:, row // 2].astype(F32)[:, 8 * (row % 2) : 8 * (row % 2) + 8].reshape(128, 128)
        e2 = jnp.concatenate([jnp.where(take_low, e, 0.0), jnp.where(take_low, 0.0, e)], axis=0).astype(BF16)
        both = mm(tb_high, e2) + mm(tb_low, e2)
        d = both[:64] + sign * pltpu.roll(both[64:], 64, 1)
        turned = pltpu.roll(d, 64, 1)
        d2 = jnp.concatenate([d, d], axis=0) * bc + jnp.concatenate([turned, turned], axis=0) * bs
        d_high, d_low = halves(d2)
        o = mm_nt(back[0], d_high) + mm_nt(back[1], d_high) + mm_nt(back[0], d_low)
        oscr[pl.ds(row, 64, stride=8), :] = o
    for v in range(64):
        out[:, 128 * v : 128 * v + 128] = oscr[pl.ds(8 * v, 8), :]
    for c in a2:
        c.wait_send()


def local(strips, facet_offset, subgrid_offset, owner, screen_index, screens, grid_weight):
    tables = [jnp.asarray(t) for t in make_tables()]
    vmem = pl.BlockSpec(memory_space=pltpu.VMEM)
    smem = pl.BlockSpec(memory_space=pltpu.SMEM)
    result = pl.pallas_call(
        kernel,
        out_shape=jax.ShapeDtypeStruct((ROWS, 2 * FL), F32),
        in_specs=[smem] * 3 + [vmem] * 10 + [pl.BlockSpec(memory_space=pl.ANY)],
        out_specs=vmem,
        scratch_shapes=[
            pltpu.VMEM((576, 128), F32),
            pltpu.VMEM((2, 128, 128), jnp.int32),
            pltpu.VMEM((2, BLOCKS, 128, 128), F32),
            pltpu.VMEM((BLOCKS, 8, 128), F32),
            pltpu.VMEM((NF, 8, 128), jnp.int32),
            pltpu.VMEM((16, ROWS, 1024), BF16),
            pltpu.VMEM((NF, 4, 16, 128), BF16),
            pltpu.VMEM((NF, 4, 16, 128), BF16),
            pltpu.VMEM((NF, 4, 16, 128), BF16),
            pltpu.VMEM((NF, 4, 16, 128), BF16),
            pltpu.VMEM((16, 128), F32),
            pltpu.VMEM((NF, 16, 128), BF16),
            pltpu.VMEM((32, 128), BF16),
            pltpu.VMEM((NS, 32, 128), BF16),
            pltpu.VMEM((576, 128), F32),
            pltpu.SemaphoreType.DMA,
            pltpu.SemaphoreType.DMA((NF - 1,)),
            pltpu.SemaphoreType.DMA((NF - 1,)),
            pltpu.SemaphoreType.DMA((NF - 1,)),
            pltpu.SemaphoreType.DMA((NF - 1,)),
            pltpu.SemaphoreType.DMA((NF - 1,)),
            pltpu.SemaphoreType.DMA((NF - 1,)),
            pltpu.SemaphoreType.DMA((NS - 1,)),
            pltpu.SemaphoreType.DMA((NS - 1,)),
        ],
        compiler_params=pltpu.CompilerParams(collective_id=0, has_side_effects=True),
        name="round_trip",
    )(
        facet_offset,
        subgrid_offset,
        screen_index,
        subgrid_offset.reshape(1, -1),
        owner.reshape(1, -1),
        strips[0],
        grid_weight,
        *tables,
        screens,
    )
    return result[None]


def solution(mesh):
    in_specs = (P("facet", "sub", None), P(), P(), P(), P(), P(), P(("facet", "sub"), None))
    out_specs = P("facet", "sub", None)
    return jax.shard_map(local, mesh=mesh, in_specs=in_specs, out_specs=out_specs, check_vma=False)
```

```python
import math

import jax
import jax.numpy as jnp
import numpy as np
from jax import lax
from jax.experimental import pallas as pl
from jax.experimental.pallas import tpu as pltpu
from jax.sharding import PartitionSpec as P

FL = 4096
CAP = 4
NF = 16
NS = 8
ROWS = 8
MINE = 8
BLOCKS = 9
SPOTS = BLOCKS * 16
MESH = pl.DeviceIdType.MESH
F32 = jnp.float32
BF16 = jnp.bfloat16


def split_halves(table):
    high = table.astype(np.float32).astype(jnp.bfloat16)
    low = (table - high.astype(np.float64)).astype(np.float32).astype(jnp.bfloat16)
    return high, low


def make_tables():
    k = np.arange(64)
    u = np.arange(32)
    b = np.arange(128)
    tau = 2.0 * np.pi
    first = tau * ((2 * k[:, None] * u[None, :]) % 64) / 64
    twist = tau * ((k[:, None] * b[None, :]) % FL) / FL
    last = tau * ((k[:, None] * b[None, :]) % 64) / 64
    scale = 1.0 / math.sqrt(FL)
    c, s = np.cos(first) * scale, np.sin(first) * scale
    ahead = np.concatenate(split_halves(np.block([[c, s], [-s, c]])), axis=1)
    cl, sl = np.cos(last), np.sin(last)
    frow = np.concatenate(split_halves(np.block([[cl, sl], [-sl, cl]])), axis=0)
    cb, sb = cl[:, :64].T, sl[:, :64].T
    brow = np.concatenate(split_halves(np.block([[cb, -sb], [sb, cb]])), axis=0)
    back = np.zeros((2, 2, 32, 2, 2, 64))
    for r in range(2):
        back[r, 0, :, 0, r], back[r, 0, :, 1, r] = c.T, -s.T
        back[r, 1, :, 0, r], back[r, 1, :, 1, r] = s.T, c.T
    back = np.concatenate(split_halves(back.reshape(128, 256)), axis=0)
    ct, st = np.cos(twist), np.sin(twist)
    twists = np.concatenate([ct, st, np.tile(ct.T, (1, 2)), np.tile(st.T, (1, 2))], axis=0).astype(np.float32)
    narrow = np.concatenate([ahead, brow], axis=0)
    wide = np.concatenate([frow, back], axis=0)
    return twists, narrow, wide


def mm(a, b):
    return jnp.dot(a, b, preferred_element_type=F32)


def mm_nt(a, b):
    return lax.dot_general(a, b, (((1,), (1,)), ((), ())), preferred_element_type=F32)


def halves(x):
    high = x.astype(BF16)
    return high, (x - high.astype(F32)).astype(BF16)


def iota(shape, dim):
    return lax.broadcasted_iota(jnp.int32, shape, dim)


def rows_of(*parts):
    return jnp.concatenate(parts, axis=0)


def lanes_of(*parts):
    return jnp.concatenate(parts, axis=1)


def both_parts(column):
    shaped = column.reshape(NF, MINE, 128)
    return jnp.concatenate([shaped, shaped], axis=1).reshape(256, 128)


def ones_where(mask):
    return jnp.where(mask, 1.0, 0.0).astype(BF16)


def kernel(
    fo_in, so_in, si_in, so_v_in, ow_v_in, strips_in, gw_in, twists_in, narrow_in, wide_in, screens, out,
    fo, so, si, so_v, ow_v, strips, gw, twists, narrow, wide, scr,
    xs, col, qsc, qfin, picks, spread, gather, low_mask, sbuf, rbuf, esend, ebuf,
    wmsg, wrows, wsend, wgot, wlow, whigh, tback, oscr,
    in_sem, scr_sem, s1, r1, s2, r2, sw1, rw1, sw2, rw2,
):
    f = lax.axis_index("facet")
    s = lax.axis_index("sub")
    fx, fy = f // 4, f % 4
    steps = [(dx, dy) for dx in range(4) for dy in range(4) if (dx, dy) != (0, 0)]
    steps.sort(key=lambda d: -(min(d[0], 4 - d[0]) + min(d[1], 4 - d[1])))
    peers = [((fx + dx) % 4) * 4 + (fy + dy) % 4 for dx, dy in steps]
    others = [(s + d) % NS for d in range(1, NS)]

    fetch = [
        pltpu.make_async_copy(a, b, in_sem.at[n])
        for n, (a, b) in enumerate(
            [
                (strips_in, strips), (so_v_in, so_v), (ow_v_in, ow_v), (narrow_in, narrow), (twists_in, twists),
                (wide_in, wide), (gw_in, gw), (fo_in, fo), (so_in, so), (si_in, si),
            ]
        )
    ]
    barrier = pltpu.get_barrier_semaphore()
    for p in peers:
        pl.semaphore_signal(barrier, inc=1, device_id=(p, s), device_id_type=MESH)
    for c in fetch:
        c.start()
    for t in others:
        pl.semaphore_signal(barrier, inc=1, device_id=(f, t), device_id_type=MESH)
    screen_copy = pltpu.make_async_copy(screens.at[:, pl.ds(pl.multiple_of(s * ROWS, ROWS), ROWS), :], scr, scr_sem)
    screen_copy.start()

    lane = iota((128, 128), 1)
    lane4 = iota((256, 128), 1)
    part4 = (iota((256, 128), 0) >> 3) & 1
    for c in fetch:
        c.wait()

    so_col = jnp.transpose(jnp.broadcast_to(so_v[...], (128, 128)))
    ow_row = jnp.broadcast_to(ow_v[...], (128, 128))
    ow_col = jnp.transpose(ow_row)
    col[...] = so_col
    start_col = (so_col + fo[f]) & (FL - 1)
    q4 = both_parts(start_col >> 6)
    take_low = (lane4 & 63) >= both_parts(start_col & 63)
    picks[:256] = ones_where(lane4 == q4 + 64 * part4)
    picks[256:] = ones_where(lane4 == ((q4 + 1) & 63) + 64 * part4)

    tf_high = mm(picks[...], wide[:128]).astype(BF16)
    tf_low = mm(picks[...], wide[128:256]).astype(BF16)
    for v in range(64):
        xs[pl.ds(8 * v, 8), :] = strips[:, 128 * v : 128 * v + 128].astype(F32)
    tc = lanes_of(twists[:64], twists[:64])
    ts = lanes_of(twists[64:128], twists[64:128])

    for h in range(2):
        columns = []
        for pair in (2 * h, 2 * h + 1):
            x = lanes_of(xs[pl.ds(2 * pair, 64, stride=8), :], xs[pl.ds(2 * pair + 1, 64, stride=8), :]).astype(BF16)
            a = mm(narrow[:128], rows_of(x, x))
            re, im = a[:64], a[64:]
            b_re = re * tc + im * ts
            b_im = im * tc - re * ts
            columns += [lanes_of(b_re[:, :128], b_im[:, :128]), lanes_of(b_re[:, 128:], b_im[:, 128:])]
        b_high, b_low = halves(rows_of(*columns))
        g = mm_nt(tf_high, b_high) + mm_nt(tf_low, b_high) + mm_nt(tf_high, b_low)
        for n in range(2):
            block = slice(128 * n, 128 * n + 128)
            piece = jnp.where(take_low, g[:256, block], g[256:, block]).astype(BF16)
            sbuf[:, 2 * h + n] = piece.reshape(NF, 16, 128)
    rbuf[pl.ds(f, 1)] = sbuf[pl.ds(f, 1)]

    for q in range(4):
        wmsg[pl.ds(4 * q, 4), :] = gw[:, 128 * q : 128 * q + 128]
    wrows[pl.ds(s, 1)] = wmsg[...].astype(BF16)[None]

    pl.semaphore_wait(barrier, NF - 1 + NS - 1)

    def remote(src, dst, send, recv, to):
        return pltpu.make_async_remote_copy(
            src_ref=src, dst_ref=dst, send_sem=send, recv_sem=recv, device_id=to, device_id_type=MESH
        )

    def everything(buffer, send, recv):
        return remote(buffer, buffer, send, recv, (peers[0], s))

    for p in peers:
        remote(sbuf.at[p], rbuf.at[f], s1, r1, (p, s)).start()
    for t in others:
        remote(wrows.at[s], wrows.at[s], sw1, rw1, (f, t)).start()

    tback[...] = mm_nt(narrow[128:], picks[...]).astype(BF16)

    lane8 = iota((8, 128), 1)
    left = lane8 < 64
    base = pl.multiple_of(f * MINE, MINE)
    r8 = col[pl.ds(base, MINE), :] & 63
    zero = jnp.zeros((8, 128), F32)
    screen_copy.wait()
    for j in range(MINE):
        shift = so[base + j] & 63
        screen = scr[si[base + j]].astype(F32)
        for part in range(2):
            rolled = [
                pltpu.roll(screen[:, 512 * part + 128 * v : 512 * part + 128 * v + 128], shift, 1) for v in range(4)
            ]
            rolled = [zero] + rolled + [zero]
            for v in range(5):
                piece = jnp.where(lane8 >= shift, rolled[v + 1], rolled[v])
                other = pltpu.roll(piece, 64, 1)
                qsc[part, 2 * v, pl.ds(j, ROWS, stride=MINE), :] = jnp.where(left, piece, other)
                if 2 * v + 1 < BLOCKS:
                    qsc[part, 2 * v + 1, pl.ds(j, ROWS, stride=MINE), :] = jnp.where(left, other, piece)
    for part in range(2):
        for b in range(BLOCKS):
            for pair in range(4):
                at = 16 * pair
                qfin[part, b, :, pl.ds(128 * pair, 128)] = jnp.where(
                    left, qsc[part, b, pl.ds(at, 8), :], qsc[part, b, pl.ds(at + 8, 8), :]
                )

    lane256 = iota((8, 256), 1)
    own = iota((8, 256), 0)
    r8w = lanes_of(r8, r8)
    for n in range(NF):
        first = ((r8w + fo[n]) >> 6) * 16 + own
        for late in range(2):
            spot = first + 16 * late
            at = 256 * late + 16 * n
            spread[pl.ds(at, 16), :] = rows_of(
                jnp.where(lane256 == spot, 1.0, 0.0), jnp.where(lane256 == spot + 8, 1.0, 0.0)
            ).astype(BF16)
        mask = jnp.where((lane8 & 63) >= ((r8 + fo[n]) & 63), 1.0, 0.0)
        low_mask[n] = rows_of(mask, mask).astype(BF16)
    unit = ones_where(iota((SPOTS, 256), 0) == iota((SPOTS, 256), 1))
    gather[...] = mm_nt(unit, spread[...]).astype(BF16)

    remote(wrows.at[pl.ds(0, NS - 1)], wrows.at[pl.ds(0, NS - 1)], sw1, rw1, (f, others[0])).wait_recv()
    all_rows = wrows[...].reshape(128, 128)
    lane64 = iota((64, 128), 1)
    sub64 = iota((64, 128), 0)
    gap = lane64 - (16 * ((sub64 >> 2) & 7) + 4 * (sub64 >> 5) + (sub64 & 3))
    lane32 = iota((32, 128), 1)
    for n in range(NF):
        offset = fo[n]
        shift = offset & 127
        rows = mm(ones_where(gap == 4 * (offset >> 7)), all_rows)
        turn = (128 - shift) & 127
        window = jnp.where(lane32 < 128 - shift, pltpu.roll(rows[:32], turn, 1), pltpu.roll(rows[32:], turn, 1))
        packed = jnp.where(lane32[:16] < 64, window[:16], pltpu.roll(window[16:], 64, 1))
        wsend[n] = packed.astype(BF16)
    wgot[pl.ds(f, 1)] = wsend[pl.ds(f, 1)]
    for p in peers:
        remote(wsend.at[p], wgot.at[f], sw2, rw2, (p, s)).start()

    everything(rbuf.at[pl.ds(0, NF - 1)], s1, r1).wait_recv()

    nothing = jnp.zeros((256 - SPOTS, 256), BF16)
    for h in range(2):
        low, high = [], []
        for pair in (2 * h, 2 * h + 1):
            c = rbuf[:, pair]
            c_low = c * low_mask[...]
            low.append(c_low.reshape(256, 128))
            high.append((c - c_low).reshape(256, 128))
        sums = mm(gather[...], rows_of(lanes_of(*low), lanes_of(*high)))
        done = []
        lanes = pl.ds(256 * h, 256)
        for b in range(BLOCKS):
            re, im = sums[16 * b : 16 * b + 8], sums[16 * b + 8 : 16 * b + 16]
            cs, sn = qfin[0, b, :, lanes], qfin[1, b, :, lanes]
            done += [re * cs - im * sn, re * sn + im * cs]
        both = mm(spread[...], rows_of(rows_of(*done).astype(BF16), nothing))
        keep = low_mask[...].reshape(256, 128) > 0
        for n in range(2):
            block = slice(128 * n, 128 * n + 128)
            piece = jnp.where(keep, both[:256, block], both[256:, block]).astype(BF16)
            esend[h, :, n] = piece.reshape(NF, 16, 128)
        for p in peers:
            remote(esend.at[h, p], ebuf.at[h, f], s2.at[h], r2.at[h], (p, s)).start()
    ebuf[:, pl.ds(f, 1)] = esend[:, pl.ds(f, 1)]

    everything(wgot.at[pl.ds(0, NF - 1)], sw2, rw2).wait_recv()
    ow_row = jnp.broadcast_to(ow_v[...], (128, 128))
    ow_col = jnp.transpose(ow_row)
    earlier = jnp.where((ow_row == ow_col) & (lane < iota((128, 128), 0)), 1.0, 0.0)
    slot = jnp.sum(earlier, axis=1, keepdims=True).astype(jnp.int32)
    weight_row = ow_col * CAP + slot
    spot = 16 * (weight_row >> 5) + (weight_row & 15)
    lane_w = iota((128, 256), 1)
    rows = mm(ones_where(lane_w == lanes_of(spot, spot)), wgot[...].reshape(256, 128))
    upper = ((weight_row >> 4) & 1) == 1
    weight = jnp.where((lane < 64) != upper, rows, pltpu.roll(rows, 64, 1))
    r_col = (col[...] + fo[f]) & 63
    for bit in range(6):
        amount = 1 << bit
        weight = jnp.where((r_col & amount) != 0, pltpu.roll(weight, amount, 1), weight)
    weight4 = both_parts(weight)
    first4 = (lane4 & 63) >= both_parts(r_col)
    wlow[...] = jnp.where(first4, weight4, 0.0).astype(BF16).reshape(NF, 16, 128)
    whigh[...] = jnp.where(first4, 0.0, weight4).astype(BF16).reshape(NF, 16, 128)

    for h in range(2):
        everything(ebuf.at[h, pl.ds(0, NF - 1)], s2.at[h], r2.at[h]).wait_recv()
        low, high = [], []
        for n in range(2):
            e = ebuf[h, :, n]
            low.append((e * wlow[...]).reshape(256, 128))
            high.append((e * whigh[...]).reshape(256, 128))
        d = mm(tback[...], rows_of(lanes_of(*low), lanes_of(*high)))
        d = d[:128] + d[128:]
        re, im = d[:64], d[64:]
        d_re, d_im = [], []
        for turn in range(2):
            at = pl.ds(128 + 64 * turn, 64)
            cs = lanes_of(twists[at, :], twists[at, :])
            at = pl.ds(256 + 64 * turn, 64)
            sn = lanes_of(twists[at, :], twists[at, :])
            d_re.append(re * cs - im * sn)
            d_im.append(re * sn + im * cs)
        d_re, d_im = rows_of(*d_re), rows_of(*d_im)
        d_high, d_low = halves(
            rows_of(lanes_of(d_re[:, :128], d_im[:, :128]), lanes_of(d_re[:, 128:], d_im[:, 128:]))
        )
        o = mm_nt(wide[256:], d_high)
        o = o[:128] + o[128:] + mm_nt(wide[256:384], d_low)
        for n in range(2):
            for r in range(2):
                oscr[pl.ds(4 * h + 2 * n + r, 64, stride=8), :] = o[64 * r : 64 * r + 64, 128 * n : 128 * n + 128]
    for v in range(64):
        out[:, 128 * v : 128 * v + 128] = oscr[pl.ds(8 * v, 8), :]

    everything(sbuf.at[pl.ds(0, NF - 1)], s1, r1).wait_send()
    everything(wsend.at[pl.ds(0, NF - 1)], sw2, rw2).wait_send()
    remote(wrows.at[pl.ds(0, NS - 1)], wrows.at[pl.ds(0, NS - 1)], sw1, rw1, (f, others[0])).wait_send()
    for h in range(2):
        everything(esend.at[h, pl.ds(0, NF - 1)], s2.at[h], r2.at[h]).wait_send()


def local(strips, facet_offset, subgrid_offset, owner, screen_index, screens, grid_weight):
    twists, narrow, wide = [jnp.asarray(t) for t in make_tables()]
    dma = pltpu.SemaphoreType.DMA
    result = pl.pallas_call(
        kernel,
        out_shape=jax.ShapeDtypeStruct((ROWS, 2 * FL), F32),
        in_specs=[pl.BlockSpec(memory_space=pl.ANY)] * 11,
        out_specs=pl.BlockSpec(memory_space=pltpu.VMEM),
        scratch_shapes=[
            pltpu.SMEM((16,), jnp.int32),
            pltpu.SMEM((128,), jnp.int32),
            pltpu.SMEM((128,), jnp.int32),
            pltpu.VMEM((1, 128), jnp.int32),
            pltpu.VMEM((1, 128), jnp.int32),
            pltpu.VMEM((ROWS, 2 * FL), BF16),
            pltpu.VMEM((CAP, 512), F32),
            pltpu.VMEM((384, 128), F32),
            pltpu.VMEM((384, 128), BF16),
            pltpu.VMEM((512, 256), BF16),
            pltpu.VMEM((16, ROWS, 1024), BF16),
            pltpu.VMEM((576, 128), F32),
            pltpu.VMEM((128, 128), jnp.int32),
            pltpu.VMEM((2, BLOCKS + 1, 128, 128), F32),
            pltpu.VMEM((2, BLOCKS, 8, 512), F32),
            pltpu.VMEM((512, 128), BF16),
            pltpu.VMEM((512, 256), BF16),
            pltpu.VMEM((SPOTS, 512), BF16),
            pltpu.VMEM((NF, 16, 128), BF16),
            pltpu.VMEM((NF, 4, 16, 128), BF16),
            pltpu.VMEM((NF, 4, 16, 128), BF16),
            pltpu.VMEM((2, NF, 2, 16, 128), BF16),
            pltpu.VMEM((2, NF, 2, 16, 128), BF16),
            pltpu.VMEM((16, 128), F32),
            pltpu.VMEM((NS, 16, 128), BF16),
            pltpu.VMEM((NF, 16, 128), BF16),
            pltpu.VMEM((NF, 16, 128), BF16),
            pltpu.VMEM((NF, 16, 128), BF16),
            pltpu.VMEM((NF, 16, 128), BF16),
            pltpu.VMEM((256, 512), BF16),
            pltpu.VMEM((576, 128), F32),
            dma((10,)), dma, dma, dma, dma((2,)), dma((2,)), dma, dma, dma, dma,
        ],
        compiler_params=pltpu.CompilerParams(collective_id=0, has_side_effects=True),
        name="round_trip",
    )(
        facet_offset,
        subgrid_offset,
        screen_index,
        subgrid_offset.reshape(1, -1),
        owner.reshape(1, -1),
        strips[0],
        grid_weight,
        twists,
        narrow,
        wide,
        screens,
    )
    return result[None]


def solution(mesh):
    in_specs = (P("facet", "sub", None), P(), P(), P(), P(), P(), P(("facet", "sub"), None))
    out_specs = P("facet", "sub", None)
    return jax.shard_map(local, mesh=mesh, in_specs=in_specs, out_specs=out_specs, check_vma=False)
```

```python
import math

import jax
import jax.numpy as jnp
import numpy as np
from jax import lax
from jax.experimental import pallas as pl
from jax.experimental.pallas import tpu as pltpu
from jax.sharding import PartitionSpec as P

FL = 4096
CAP = 4
NF = 16
NS = 8
ROWS = 8
MINE = 8
BLOCKS = 9
SPOTS = BLOCKS * 16
MESH = pl.DeviceIdType.MESH
F32 = jnp.float32
BF16 = jnp.bfloat16


def split_halves(table):
    high = table.astype(np.float32).astype(jnp.bfloat16)
    low = (table - high.astype(np.float64)).astype(np.float32).astype(jnp.bfloat16)
    return high, low


def make_tables():
    k = np.arange(64)
    u = np.arange(32)
    b = np.arange(128)
    tau = 2.0 * np.pi
    first = tau * ((2 * k[:, None] * u[None, :]) % 64) / 64
    twist = tau * ((k[:, None] * b[None, :]) % FL) / FL
    last = tau * ((k[:, None] * b[None, :]) % 64) / 64
    scale = 1.0 / math.sqrt(FL)
    c, s = np.cos(first) * scale, np.sin(first) * scale
    ahead = np.concatenate(split_halves(np.block([[c, s], [-s, c]])), axis=1)
    cl, sl = np.cos(last), np.sin(last)
    frow = np.concatenate(split_halves(np.block([[cl, sl], [-sl, cl]])), axis=0)
    cb, sb = cl[:, :64].T, sl[:, :64].T
    brow = np.concatenate(split_halves(np.block([[cb, -sb], [sb, cb]])), axis=0)
    back = np.zeros((2, 2, 32, 2, 2, 64))
    for r in range(2):
        back[r, 0, :, 0, r], back[r, 0, :, 1, r] = c.T, -s.T
        back[r, 1, :, 0, r], back[r, 1, :, 1, r] = s.T, c.T
    back = np.concatenate(split_halves(back.reshape(128, 256)), axis=0)
    ct, st = np.cos(twist), np.sin(twist)
    twists = np.concatenate([ct, st, np.tile(ct.T, (1, 2)), np.tile(st.T, (1, 2))], axis=0).astype(np.float32)
    narrow = np.concatenate([ahead, brow], axis=0)
    wide = np.concatenate([frow, back], axis=0)
    return twists, narrow, wide


def mm(a, b):
    return jnp.dot(a, b, preferred_element_type=F32)


def mm_nt(a, b):
    return lax.dot_general(a, b, (((1,), (1,)), ((), ())), preferred_element_type=F32)


def halves(x):
    high = x.astype(BF16)
    return high, (x - high.astype(F32)).astype(BF16)


def iota(shape, dim):
    return lax.broadcasted_iota(jnp.int32, shape, dim)


def rows_of(*parts):
    return jnp.concatenate(parts, axis=0)


def lanes_of(*parts):
    return jnp.concatenate(parts, axis=1)


def both_parts(column):
    shaped = column.reshape(NF, MINE, 128)
    return jnp.concatenate([shaped, shaped], axis=1).reshape(256, 128)


def ones_where(mask):
    return jnp.where(mask, 1.0, 0.0).astype(BF16)


def kernel(
    fo_in, so_in, si_in, so_v_in, ow_v_in, strips_in, gw_in, twists_in, narrow_in, wide_in, screens, out,
    fo, so, si, so_v, ow_v, strips, gw, twists, narrow, wide, scr,
    xs, col, qsc, qfin, picks, spread, gather, low_mask, sbuf, rbuf, esend, ebuf,
    wmsg, wrows, wsend, wgot, wlow, whigh, tback, oscr,
    in_sem, scr_sem, s1, r1, s2, r2, sw1, rw1, sw2, rw2,
):
    f = lax.axis_index("facet")
    s = lax.axis_index("sub")
    fx, fy = f // 4, f % 4
    steps = [(dx, dy) for dx in range(4) for dy in range(4) if (dx, dy) != (0, 0)]
    steps.sort(key=lambda d: -(min(d[0], 4 - d[0]) + min(d[1], 4 - d[1])))
    peers = [((fx + dx) % 4) * 4 + (fy + dy) % 4 for dx, dy in steps]
    others = [(s + d) % NS for d in range(1, NS)]

    fetch = [
        pltpu.make_async_copy(a, b, in_sem.at[n])
        for n, (a, b) in enumerate(
            [
                (strips_in, strips), (so_v_in, so_v), (ow_v_in, ow_v), (narrow_in, narrow), (twists_in, twists),
                (wide_in, wide), (gw_in, gw), (fo_in, fo), (so_in, so), (si_in, si),
            ]
        )
    ]
    barrier = pltpu.get_barrier_semaphore()
    for p in peers:
        pl.semaphore_signal(barrier, inc=1, device_id=(p, s), device_id_type=MESH)
    for c in fetch:
        c.start()
    for t in others:
        pl.semaphore_signal(barrier, inc=1, device_id=(f, t), device_id_type=MESH)
    screen_copy = pltpu.make_async_copy(screens.at[:, pl.ds(pl.multiple_of(s * ROWS, ROWS), ROWS), :], scr, scr_sem)
    screen_copy.start()

    lane = iota((128, 128), 1)
    lane4 = iota((256, 128), 1)
    part4 = (iota((256, 128), 0) >> 3) & 1
    for c in fetch:
        c.wait()

    so_col = jnp.transpose(jnp.broadcast_to(so_v[...], (128, 128)))
    ow_row = jnp.broadcast_to(ow_v[...], (128, 128))
    ow_col = jnp.transpose(ow_row)
    col[...] = so_col
    start_col = (so_col + fo[f]) & (FL - 1)
    q4 = both_parts(start_col >> 6)
    take_low = (lane4 & 63) >= both_parts(start_col & 63)
    picks[:256] = ones_where(lane4 == q4 + 64 * part4)
    picks[256:] = ones_where(lane4 == ((q4 + 1) & 63) + 64 * part4)

    tf_high = mm(picks[...], wide[:128]).astype(BF16)
    tf_low = mm(picks[...], wide[128:256]).astype(BF16)
    for v in range(64):
        xs[pl.ds(8 * v, 8), :] = strips[:, 128 * v : 128 * v + 128].astype(F32)
    tc = lanes_of(twists[:64], twists[:64])
    ts = lanes_of(twists[64:128], twists[64:128])

    for h in range(2):
        columns = []
        for pair in (2 * h, 2 * h + 1):
            x = lanes_of(xs[pl.ds(2 * pair, 64, stride=8), :], xs[pl.ds(2 * pair + 1, 64, stride=8), :]).astype(BF16)
            a = mm(narrow[:128], rows_of(x, x))
            re, im = a[:64], a[64:]
            b_re = re * tc + im * ts
            b_im = im * tc - re * ts
            columns += [lanes_of(b_re[:, :128], b_im[:, :128]), lanes_of(b_re[:, 128:], b_im[:, 128:])]
        b_high, b_low = halves(rows_of(*columns))
        g = mm_nt(tf_high, b_high) + mm_nt(tf_low, b_high) + mm_nt(tf_high, b_low)
        for n in range(2):
            block = slice(128 * n, 128 * n + 128)
            piece = jnp.where(take_low, g[:256, block], g[256:, block]).astype(BF16)
            sbuf[:, 2 * h + n] = piece.reshape(NF, 16, 128)
    rbuf[pl.ds(f, 1)] = sbuf[pl.ds(f, 1)]

    for q in range(4):
        wmsg[pl.ds(4 * q, 4), :] = gw[:, 128 * q : 128 * q + 128]
    wrows[pl.ds(s, 1)] = wmsg[...].astype(BF16)[None]

    pl.semaphore_wait(barrier, NF - 1 + NS - 1)

    def remote(src, dst, send, recv, to):
        return pltpu.make_async_remote_copy(
            src_ref=src, dst_ref=dst, send_sem=send, recv_sem=recv, device_id=to, device_id_type=MESH
        )

    def everything(buffer, send, recv):
        return remote(buffer, buffer, send, recv, (peers[0], s))

    for p in peers:
        remote(sbuf.at[p], rbuf.at[f], s1, r1, (p, s)).start()
    for t in others:
        remote(wrows.at[s], wrows.at[s], sw1, rw1, (f, t)).start()

    tback[...] = mm_nt(narrow[128:], picks[...]).astype(BF16)

    lane8 = iota((8, 128), 1)
    left = lane8 < 64
    base = pl.multiple_of(f * MINE, MINE)
    r8 = col[pl.ds(base, MINE), :] & 63
    zero = jnp.zeros((8, 128), F32)
    screen_copy.wait()
    for j in range(MINE):
        shift = so[base + j] & 63
        screen = scr[si[base + j]].astype(F32)
        for part in range(2):
            rolled = [
                pltpu.roll(screen[:, 512 * part + 128 * v : 512 * part + 128 * v + 128], shift, 1) for v in range(4)
            ]
            rolled = [zero] + rolled + [zero]
            for v in range(5):
                piece = jnp.where(lane8 >= shift, rolled[v + 1], rolled[v])
                other = pltpu.roll(piece, 64, 1)
                qsc[part, 2 * v, pl.ds(j, ROWS, stride=MINE), :] = jnp.where(left, piece, other)
                if 2 * v + 1 < BLOCKS:
                    qsc[part, 2 * v + 1, pl.ds(j, ROWS, stride=MINE), :] = jnp.where(left, other, piece)
    for part in range(2):
        for b in range(BLOCKS):
            for pair in range(4):
                at = 16 * pair
                qfin[part, b, :, pl.ds(128 * pair, 128)] = jnp.where(
                    left, qsc[part, b, pl.ds(at, 8), :], qsc[part, b, pl.ds(at + 8, 8), :]
                )

    lane256 = iota((8, 256), 1)
    own = iota((8, 256), 0)
    r8w = lanes_of(r8, r8)
    for n in range(NF):
        first = ((r8w + fo[n]) >> 6) * 16 + own
        for late in range(2):
            spot = first + 16 * late
            at = 256 * late + 16 * n
            spread[pl.ds(at, 16), :] = rows_of(
                jnp.where(lane256 == spot, 1.0, 0.0), jnp.where(lane256 == spot + 8, 1.0, 0.0)
            ).astype(BF16)
        mask = jnp.where((lane8 & 63) >= ((r8 + fo[n]) & 63), 1.0, 0.0)
        low_mask[n] = rows_of(mask, mask).astype(BF16)
    unit = ones_where(iota((SPOTS, 256), 0) == iota((SPOTS, 256), 1))
    gather[...] = mm_nt(unit, spread[...]).astype(BF16)

    remote(wrows.at[pl.ds(0, NS - 1)], wrows.at[pl.ds(0, NS - 1)], sw1, rw1, (f, others[0])).wait_recv()
    all_rows = wrows[...].reshape(128, 128)
    lane64 = iota((64, 128), 1)
    sub64 = iota((64, 128), 0)
    gap = lane64 - (16 * ((sub64 >> 2) & 7) + 4 * (sub64 >> 5) + (sub64 & 3))
    lane32 = iota((32, 128), 1)
    for n in range(NF):
        offset = fo[n]
        shift = offset & 127
        rows = mm(ones_where(gap == 4 * (offset >> 7)), all_rows)
        turn = (128 - shift) & 127
        window = jnp.where(lane32 < 128 - shift, pltpu.roll(rows[:32], turn, 1), pltpu.roll(rows[32:], turn, 1))
        packed = jnp.where(lane32[:16] < 64, window[:16], pltpu.roll(window[16:], 64, 1))
        wsend[n] = packed.astype(BF16)
    wgot[pl.ds(f, 1)] = wsend[pl.ds(f, 1)]
    for p in peers:
        remote(wsend.at[p], wgot.at[f], sw2, rw2, (p, s)).start()

    everything(rbuf.at[pl.ds(0, NF - 1)], s1, r1).wait_recv()

    nothing = jnp.zeros((256 - SPOTS, 256), BF16)
    for h in range(2):
        low, high = [], []
        for pair in (2 * h, 2 * h + 1):
            c = rbuf[:, pair]
            c_low = c * low_mask[...]
            low.append(c_low.reshape(256, 128))
            high.append((c - c_low).reshape(256, 128))
        sums = mm(gather[...], rows_of(lanes_of(*low), lanes_of(*high)))
        done = []
        lanes = pl.ds(256 * h, 256)
        for b in range(BLOCKS):
            re, im = sums[16 * b : 16 * b + 8], sums[16 * b + 8 : 16 * b + 16]
            cs, sn = qfin[0, b, :, lanes], qfin[1, b, :, lanes]
            done += [re * cs - im * sn, re * sn + im * cs]
        both = mm(spread[...], rows_of(rows_of(*done).astype(BF16), nothing))
        keep = low_mask[...].reshape(256, 128) > 0
        for n in range(2):
            block = slice(128 * n, 128 * n + 128)
            piece = jnp.where(keep, both[:256, block], both[256:, block]).astype(BF16)
            esend[h, :, n] = piece.reshape(NF, 16, 128)
        for p in peers:
            remote(esend.at[h, p], ebuf.at[h, f], s2.at[h], r2.at[h], (p, s)).start()
    ebuf[:, pl.ds(f, 1)] = esend[:, pl.ds(f, 1)]

    everything(wgot.at[pl.ds(0, NF - 1)], sw2, rw2).wait_recv()
    ow_row = jnp.broadcast_to(ow_v[...], (128, 128))
    ow_col = jnp.transpose(ow_row)
    earlier = jnp.where((ow_row == ow_col) & (lane < iota((128, 128), 0)), 1.0, 0.0)
    slot = jnp.sum(earlier, axis=1, keepdims=True).astype(jnp.int32)
    weight_row = ow_col * CAP + slot
    spot = 16 * (weight_row >> 5) + (weight_row & 15)
    lane_w = iota((128, 256), 1)
    rows = mm(ones_where(lane_w == lanes_of(spot, spot)), wgot[...].reshape(256, 128))
    upper = ((weight_row >> 4) & 1) == 1
    weight = jnp.where((lane < 64) != upper, rows, pltpu.roll(rows, 64, 1))
    r_col = (col[...] + fo[f]) & 63
    for bit in range(6):
        amount = 1 << bit
        weight = jnp.where((r_col & amount) != 0, pltpu.roll(weight, amount, 1), weight)
    weight4 = both_parts(weight)
    first4 = (lane4 & 63) >= both_parts(r_col)
    wlow[...] = jnp.where(first4, weight4, 0.0).astype(BF16).reshape(NF, 16, 128)
    whigh[...] = jnp.where(first4, 0.0, weight4).astype(BF16).reshape(NF, 16, 128)

    for h in range(2):
        everything(ebuf.at[h, pl.ds(0, NF - 1)], s2.at[h], r2.at[h]).wait_recv()
        low, high = [], []
        for n in range(2):
            e = ebuf[h, :, n]
            low.append((e * wlow[...]).reshape(256, 128))
            high.append((e * whigh[...]).reshape(256, 128))
        d = mm(tback[...], rows_of(lanes_of(*low), lanes_of(*high)))
        d = d[:128] + d[128:]
        re, im = d[:64], d[64:]
        d_re, d_im = [], []
        for turn in range(2):
            at = pl.ds(128 + 64 * turn, 64)
            cs = lanes_of(twists[at, :], twists[at, :])
            at = pl.ds(256 + 64 * turn, 64)
            sn = lanes_of(twists[at, :], twists[at, :])
            d_re.append(re * cs - im * sn)
            d_im.append(re * sn + im * cs)
        d_re, d_im = rows_of(*d_re), rows_of(*d_im)
        d_high, d_low = halves(
            rows_of(lanes_of(d_re[:, :128], d_im[:, :128]), lanes_of(d_re[:, 128:], d_im[:, 128:]))
        )
        o = mm_nt(wide[256:], d_high)
        o = o[:128] + o[128:] + mm_nt(wide[256:384], d_low)
        for n in range(2):
            for r in range(2):
                oscr[pl.ds(4 * h + 2 * n + r, 64, stride=8), :] = o[64 * r : 64 * r + 64, 128 * n : 128 * n + 128]
    for v in range(64):
        out[:, 128 * v : 128 * v + 128] = oscr[pl.ds(8 * v, 8), :]

    everything(sbuf.at[pl.ds(0, NF - 1)], s1, r1).wait_send()
    everything(wsend.at[pl.ds(0, NF - 1)], sw2, rw2).wait_send()
    remote(wrows.at[pl.ds(0, NS - 1)], wrows.at[pl.ds(0, NS - 1)], sw1, rw1, (f, others[0])).wait_send()
    for h in range(2):
        everything(esend.at[h, pl.ds(0, NF - 1)], s2.at[h], r2.at[h]).wait_send()


def local(strips, facet_offset, subgrid_offset, owner, screen_index, screens, grid_weight):
    twists, narrow, wide = [jnp.asarray(t) for t in make_tables()]
    dma = pltpu.SemaphoreType.DMA
    result = pl.pallas_call(
        kernel,
        out_shape=jax.ShapeDtypeStruct((ROWS, 2 * FL), F32),
        in_specs=[pl.BlockSpec(memory_space=pltpu.HBM)] * 11,
        out_specs=pl.BlockSpec(memory_space=pltpu.VMEM),
        scratch_shapes=[
            pltpu.SMEM((16,), jnp.int32),
            pltpu.SMEM((128,), jnp.int32),
            pltpu.SMEM((128,), jnp.int32),
            pltpu.VMEM((1, 128), jnp.int32),
            pltpu.VMEM((1, 128), jnp.int32),
            pltpu.VMEM((ROWS, 2 * FL), BF16),
            pltpu.VMEM((CAP, 512), F32),
            pltpu.VMEM((384, 128), F32),
            pltpu.VMEM((384, 128), BF16),
            pltpu.VMEM((512, 256), BF16),
            pltpu.VMEM((16, ROWS, 1024), BF16),
            pltpu.VMEM((576, 128), F32),
            pltpu.VMEM((128, 128), jnp.int32),
            pltpu.VMEM((2, BLOCKS + 1, 128, 128), F32),
            pltpu.VMEM((2, BLOCKS, 8, 512), F32),
            pltpu.VMEM((512, 128), BF16),
            pltpu.VMEM((512, 256), BF16),
            pltpu.VMEM((SPOTS, 512), BF16),
            pltpu.VMEM((NF, 16, 128), BF16),
            pltpu.VMEM((NF, 4, 16, 128), BF16),
            pltpu.VMEM((NF, 4, 16, 128), BF16),
            pltpu.VMEM((2, NF, 2, 16, 128), BF16),
            pltpu.VMEM((2, NF, 2, 16, 128), BF16),
            pltpu.VMEM((16, 128), F32),
            pltpu.VMEM((NS, 16, 128), BF16),
            pltpu.VMEM((NF, 16, 128), BF16),
            pltpu.VMEM((NF, 16, 128), BF16),
            pltpu.VMEM((NF, 16, 128), BF16),
            pltpu.VMEM((NF, 16, 128), BF16),
            pltpu.VMEM((256, 512), BF16),
            pltpu.VMEM((576, 128), F32),
            dma((10,)), dma, dma, dma, dma((2,)), dma((2,)), dma, dma, dma, dma,
        ],
        compiler_params=pltpu.CompilerParams(collective_id=0, has_side_effects=True, vmem_limit_bytes=16*1024*1024),
        name="round_trip",
    )(
        *[
            pltpu.with_memory_space_constraint(a, pltpu.HBM)
            for a in (
                facet_offset, subgrid_offset, screen_index, subgrid_offset.reshape(1, -1), owner.reshape(1, -1),
                strips[0], grid_weight, twists, narrow, wide, screens,
            )
        ]
    )
    return result[None]


def solution(mesh):
    in_specs = (P("facet", "sub", None), P(), P(), P(), P(), P(), P(("facet", "sub"), None))
    out_specs = P("facet", "sub", None)
    return jax.shard_map(local, mesh=mesh, in_specs=in_specs, out_specs=out_specs, check_vma=False)
```

```python
import math

import jax
import jax.numpy as jnp
import numpy as np
from jax import lax
from jax.experimental import pallas as pl
from jax.experimental.pallas import tpu as pltpu
from jax.sharding import PartitionSpec as P

FL = 4096
CAP = 4
NF = 16
NS = 8
ROWS = 8
MINE = 8
BLOCKS = 9
SPOTS = BLOCKS * 16
MESH = pl.DeviceIdType.MESH
F32 = jnp.float32
BF16 = jnp.bfloat16


def split_halves(table):
    high = table.astype(np.float32).astype(jnp.bfloat16)
    low = (table - high.astype(np.float64)).astype(np.float32).astype(jnp.bfloat16)
    return high, low


def make_tables():
    k = np.arange(64)
    u = np.arange(32)
    b = np.arange(128)
    tau = 2.0 * np.pi
    first = tau * ((2 * k[:, None] * u[None, :]) % 64) / 64
    twist = tau * ((k[:, None] * b[None, :]) % FL) / FL
    last = tau * ((k[:, None] * b[None, :]) % 64) / 64
    scale = 1.0 / math.sqrt(FL)
    c, s = np.cos(first) * scale, np.sin(first) * scale
    ahead = np.concatenate(split_halves(np.block([[c, s], [-s, c]])), axis=1)
    cl, sl = np.cos(last), np.sin(last)
    frow = np.concatenate(split_halves(np.block([[cl, sl], [-sl, cl]])), axis=0)
    cb, sb = cl[:, :64].T, sl[:, :64].T
    brow = np.concatenate(split_halves(np.block([[cb, -sb], [sb, cb]])), axis=0)
    back = np.zeros((2, 2, 32, 2, 2, 64))
    for r in range(2):
        back[r, 0, :, 0, r], back[r, 0, :, 1, r] = c.T, -s.T
        back[r, 1, :, 0, r], back[r, 1, :, 1, r] = s.T, c.T
    back = np.concatenate(split_halves(back.reshape(128, 256)), axis=0)
    ct, st = np.cos(twist), np.sin(twist)
    twists = np.concatenate([ct, st, np.tile(ct.T, (1, 2)), np.tile(st.T, (1, 2))], axis=0).astype(np.float32)
    narrow = np.concatenate([ahead, brow], axis=0)
    wide = np.concatenate([frow, back], axis=0)
    return twists, narrow, wide


def mm(a, b):
    return jnp.dot(a, b, preferred_element_type=F32)


def mm_nt(a, b):
    return lax.dot_general(a, b, (((1,), (1,)), ((), ())), preferred_element_type=F32)


def halves(x):
    high = x.astype(BF16)
    return high, (x - high.astype(F32)).astype(BF16)


def iota(shape, dim):
    return lax.broadcasted_iota(jnp.int32, shape, dim)


def rows_of(*parts):
    return jnp.concatenate(parts, axis=0)


def lanes_of(*parts):
    return jnp.concatenate(parts, axis=1)


def both_parts(column):
    shaped = column.reshape(NF, MINE, 128)
    return jnp.concatenate([shaped, shaped], axis=1).reshape(256, 128)


def ones_where(mask):
    return jnp.where(mask, 1.0, 0.0).astype(BF16)


def kernel(
    fo_in, so_in, si_in, so_v_in, ow_v_in, strips_in, gw_in, twists_in, narrow_in, wide_in, screens, out,
    fo, so, si, so_v, ow_v, strips, gw, gwq, twists, narrow, wide, scr,
    xs, col, qsc, qfin, picks, spread, gather, low_mask, sbuf, rbuf, esend, ebuf,
    wout, wgot, chosen, wlow, whigh, tback, oscr,
    in_sem, scr_sem, known, s1, r1, s2, r2, sw1, rw1, sw2, rw2,
):
    f = lax.axis_index("facet")
    s = lax.axis_index("sub")
    fx, fy = f // 4, f % 4
    steps = [(dx, dy) for dx in range(4) for dy in range(4) if (dx, dy) != (0, 0)]
    steps.sort(key=lambda d: -(min(d[0], 4 - d[0]) + min(d[1], 4 - d[1])))
    peers = [((fx + dx) % 4) * 4 + (fy + dy) % 4 for dx, dy in steps]

    fetch = [
        pltpu.make_async_copy(a, b, in_sem.at[n])
        for n, (a, b) in enumerate(
            [
                (strips_in, strips), (so_v_in, so_v), (ow_v_in, ow_v), (narrow_in, narrow), (twists_in, twists),
                (wide_in, wide), (gw_in, gw), (fo_in, fo), (so_in, so), (si_in, si),
            ]
        )
    ]
    barrier = pltpu.get_barrier_semaphore()
    for p in peers:
        pl.semaphore_signal(barrier, inc=1, device_id=(p, s), device_id_type=MESH)
    for c in fetch:
        c.start()

    def greet(t, carry):
        pl.semaphore_signal(barrier, inc=1, device_id=(f, t), device_id_type=MESH)
        return carry

    lax.fori_loop(s + 1, NS, greet, 0)
    screen_copy = pltpu.make_async_copy(screens.at[:, pl.ds(pl.multiple_of(s * ROWS, ROWS), ROWS), :], scr, scr_sem)
    screen_copy.start()

    lane = iota((128, 128), 1)
    lane4 = iota((256, 128), 1)
    part4 = (iota((256, 128), 0) >> 3) & 1
    for c in fetch:
        c.wait()

    so_col = jnp.transpose(jnp.broadcast_to(so_v[...], (128, 128)))
    ow_row = jnp.broadcast_to(ow_v[...], (128, 128))
    ow_col = jnp.transpose(ow_row)
    col[...] = so_col
    start_col = (so_col + fo[f]) & (FL - 1)
    q4 = both_parts(start_col >> 6)
    take_low = (lane4 & 63) >= both_parts(start_col & 63)
    picks[:256] = ones_where(lane4 == q4 + 64 * part4)
    picks[256:] = ones_where(lane4 == ((q4 + 1) & 63) + 64 * part4)

    tf_high = mm(picks[...], wide[:128]).astype(BF16)
    tf_low = mm(picks[...], wide[128:256]).astype(BF16)
    for v in range(64):
        xs[pl.ds(8 * v, 8), :] = strips[:, 128 * v : 128 * v + 128].astype(F32)
    tc = lanes_of(twists[:64], twists[:64])
    ts = lanes_of(twists[64:128], twists[64:128])

    for h in range(2):
        columns = []
        for pair in (2 * h, 2 * h + 1):
            x = lanes_of(xs[pl.ds(2 * pair, 64, stride=8), :], xs[pl.ds(2 * pair + 1, 64, stride=8), :]).astype(BF16)
            a = mm(narrow[:128], rows_of(x, x))
            re, im = a[:64], a[64:]
            b_re = re * tc + im * ts
            b_im = im * tc - re * ts
            columns += [lanes_of(b_re[:, :128], b_im[:, :128]), lanes_of(b_re[:, 128:], b_im[:, 128:])]
        b_high, b_low = halves(rows_of(*columns))
        g = mm_nt(tf_high, b_high) + mm_nt(tf_low, b_high) + mm_nt(tf_high, b_low)
        for n in range(2):
            block = slice(128 * n, 128 * n + 128)
            piece = jnp.where(take_low, g[:256, block], g[256:, block]).astype(BF16)
            sbuf[:, 2 * h + n] = piece.reshape(NF, 16, 128)
    rbuf[pl.ds(f, 1)] = sbuf[pl.ds(f, 1)]

    lane_cap = iota((8, 128), 1)
    gwq[...] = jnp.zeros((5, 8, 128), F32)
    for q in range(4):
        gwq[q, pl.ds(0, CAP), :] = gw[:, 128 * q : 128 * q + 128]
    for n in range(NF):
        shift = fo[n] & 127
        block = fo[n] >> 7
        turn = (128 - shift) & 127
        window = jnp.where(
            lane_cap < 128 - shift, pltpu.roll(gwq[block], turn, 1), pltpu.roll(gwq[block + 1], turn, 1)
        )
        beside = pltpu.roll(pltpu.roll(window, 6, 0), 64, 1)
        wout[n] = jnp.where(lane_cap < 64, window, beside)[:2].astype(BF16)
    wgot[pl.ds(s, 1), pl.ds(f, 1)] = wout[pl.ds(f, 1)][None]

    pl.semaphore_wait(barrier, NF - 1 + s)

    def remote(src, dst, send, recv, to):
        return pltpu.make_async_remote_copy(
            src_ref=src, dst_ref=dst, send_sem=send, recv_sem=recv, device_id=to, device_id_type=MESH
        )

    def everything(buffer, send, recv):
        return remote(buffer, buffer, send, recv, (peers[0], s))

    for p in peers:
        remote(wout.at[p], wgot.at[s, f], sw1, rw1, (p, s)).start()
    for p in peers:
        remote(sbuf.at[p], rbuf.at[f], s1, r1, (p, s)).start()

    def tell(t, carry):
        pl.semaphore_signal(known.at[s], inc=1, device_id=(f, t), device_id_type=MESH)
        return carry

    def hear(t, carry):
        pl.semaphore_wait(known.at[t], 1)
        return carry

    def weights_to(t, carry):
        remote(wgot.at[s], wgot.at[s], sw2, rw2, (f, t)).start()
        return carry

    lax.fori_loop(0, s, tell, 0)

    tback[...] = mm_nt(narrow[128:], picks[...]).astype(BF16)

    lane8 = iota((8, 128), 1)
    left = lane8 < 64
    base = pl.multiple_of(f * MINE, MINE)
    r8 = col[pl.ds(base, MINE), :] & 63
    zero = jnp.zeros((8, 128), F32)
    screen_copy.wait()
    for j in range(MINE):
        shift = so[base + j] & 63
        screen = scr[si[base + j]].astype(F32)
        for part in range(2):
            rolled = [
                pltpu.roll(screen[:, 512 * part + 128 * v : 512 * part + 128 * v + 128], shift, 1) for v in range(4)
            ]
            rolled = [zero] + rolled + [zero]
            for v in range(5):
                piece = jnp.where(lane8 >= shift, rolled[v + 1], rolled[v])
                other = pltpu.roll(piece, 64, 1)
                qsc[part, 2 * v, pl.ds(j, ROWS, stride=MINE), :] = jnp.where(left, piece, other)
                if 2 * v + 1 < BLOCKS:
                    qsc[part, 2 * v + 1, pl.ds(j, ROWS, stride=MINE), :] = jnp.where(left, other, piece)
    for part in range(2):
        for b in range(BLOCKS):
            for pair in range(4):
                at = 16 * pair
                qfin[part, b, :, pl.ds(128 * pair, 128)] = jnp.where(
                    left, qsc[part, b, pl.ds(at, 8), :], qsc[part, b, pl.ds(at + 8, 8), :]
                )

    lane256 = iota((8, 256), 1)
    own = iota((8, 256), 0)
    r8w = lanes_of(r8, r8)
    for n in range(NF):
        first = ((r8w + fo[n]) >> 6) * 16 + own
        for late in range(2):
            spot = first + 16 * late
            at = 256 * late + 16 * n
            spread[pl.ds(at, 16), :] = rows_of(
                jnp.where(lane256 == spot, 1.0, 0.0), jnp.where(lane256 == spot + 8, 1.0, 0.0)
            ).astype(BF16)
        mask = jnp.where((lane8 & 63) >= ((r8 + fo[n]) & 63), 1.0, 0.0)
        low_mask[n] = rows_of(mask, mask).astype(BF16)
    unit = ones_where(iota((SPOTS, 256), 0) == iota((SPOTS, 256), 1))
    gather[...] = mm_nt(unit, spread[...]).astype(BF16)

    everything(wgot.at[0, pl.ds(0, NF - 1)], sw1, rw1).wait_recv()
    lax.fori_loop(0, s, weights_to, 0)

    everything(rbuf.at[pl.ds(0, NF - 1)], s1, r1).wait_recv()

    nothing = jnp.zeros((256 - SPOTS, 256), BF16)
    for h in range(2):
        low, high = [], []
        for pair in (2 * h, 2 * h + 1):
            c = rbuf[:, pair]
            c_low = c * low_mask[...]
            low.append(c_low.reshape(256, 128))
            high.append((c - c_low).reshape(256, 128))
        sums = mm(gather[...], rows_of(lanes_of(*low), lanes_of(*high)))
        done = []
        lanes = pl.ds(256 * h, 256)
        for b in range(BLOCKS):
            re, im = sums[16 * b : 16 * b + 8], sums[16 * b + 8 : 16 * b + 16]
            cs, sn = qfin[0, b, :, lanes], qfin[1, b, :, lanes]
            done += [re * cs - im * sn, re * sn + im * cs]
        both = mm(spread[...], rows_of(rows_of(*done).astype(BF16), nothing))
        keep = low_mask[...].reshape(256, 128) > 0
        for n in range(2):
            block = slice(128 * n, 128 * n + 128)
            piece = jnp.where(keep, both[:256, block], both[256:, block]).astype(BF16)
            esend[h, :, n] = piece.reshape(NF, 16, 128)
        for p in peers:
            remote(esend.at[h, p], ebuf.at[h, f], s2.at[h], r2.at[h], (p, s)).start()
    ebuf[:, pl.ds(f, 1)] = esend[:, pl.ds(f, 1)]

    lax.fori_loop(s + 1, NS, hear, 0)
    lax.fori_loop(s + 1, NS, weights_to, 0)

    ow_row = jnp.broadcast_to(ow_v[...], (128, 128))
    ow_col = jnp.transpose(ow_row)
    earlier = jnp.where((ow_row == ow_col) & (lane < iota((128, 128), 0)), 1.0, 0.0)
    slot = jnp.sum(earlier, axis=1, keepdims=True).astype(jnp.int32)
    weight_row = ow_col * CAP + slot
    spot = 32 * ((weight_row >> 2) & 7) + 2 * (weight_row >> 5) + (weight_row & 1)
    chosen[...] = ones_where(iota((128, 256), 1) == lanes_of(spot, spot))
    upper = (weight_row & 2) == 2
    r_col = (col[...] + fo[f]) & 63
    everything(wgot.at[pl.ds(0, NS - 1)], sw2, rw2).wait_recv()
    rows = mm(chosen[...], wgot[...].reshape(256, 128))
    weight = jnp.where((lane < 64) != upper, rows, pltpu.roll(rows, 64, 1))
    for bit in range(6):
        amount = 1 << bit
        weight = jnp.where((r_col & amount) != 0, pltpu.roll(weight, amount, 1), weight)
    weight4 = both_parts(weight)
    first4 = (lane4 & 63) >= both_parts(r_col)
    wlow[...] = jnp.where(first4, weight4, 0.0).astype(BF16).reshape(NF, 16, 128)
    whigh[...] = jnp.where(first4, 0.0, weight4).astype(BF16).reshape(NF, 16, 128)

    for h in range(2):
        everything(ebuf.at[h, pl.ds(0, NF - 1)], s2.at[h], r2.at[h]).wait_recv()
        low, high = [], []
        for n in range(2):
            e = ebuf[h, :, n]
            low.append((e * wlow[...]).reshape(256, 128))
            high.append((e * whigh[...]).reshape(256, 128))
        d = mm(tback[...], rows_of(lanes_of(*low), lanes_of(*high)))
        d = d[:128] + d[128:]
        re, im = d[:64], d[64:]
        d_re, d_im = [], []
        for turn in range(2):
            at = pl.ds(128 + 64 * turn, 64)
            cs = lanes_of(twists[at, :], twists[at, :])
            at = pl.ds(256 + 64 * turn, 64)
            sn = lanes_of(twists[at, :], twists[at, :])
            d_re.append(re * cs - im * sn)
            d_im.append(re * sn + im * cs)
        d_re, d_im = rows_of(*d_re), rows_of(*d_im)
        d_high, d_low = halves(
            rows_of(lanes_of(d_re[:, :128], d_im[:, :128]), lanes_of(d_re[:, 128:], d_im[:, 128:]))
        )
        o = mm_nt(wide[256:], d_high)
        o = o[:128] + o[128:] + mm_nt(wide[256:384], d_low)
        for n in range(2):
            for r in range(2):
                oscr[pl.ds(4 * h + 2 * n + r, 64, stride=8), :] = o[64 * r : 64 * r + 64, 128 * n : 128 * n + 128]
    for v in range(64):
        out[:, 128 * v : 128 * v + 128] = oscr[pl.ds(8 * v, 8), :]

    everything(sbuf.at[pl.ds(0, NF - 1)], s1, r1).wait_send()
    everything(wout.at[pl.ds(0, NF - 1)], sw1, rw1).wait_send()
    everything(wgot.at[pl.ds(0, NS - 1)], sw2, rw2).wait_send()
    for h in range(2):
        everything(esend.at[h, pl.ds(0, NF - 1)], s2.at[h], r2.at[h]).wait_send()


def local(strips, facet_offset, subgrid_offset, owner, screen_index, screens, grid_weight):
    twists, narrow, wide = [jnp.asarray(t) for t in make_tables()]
    dma = pltpu.SemaphoreType.DMA
    result = pl.pallas_call(
        kernel,
        out_shape=jax.ShapeDtypeStruct((ROWS, 2 * FL), F32),
        in_specs=[pl.BlockSpec(memory_space=pltpu.HBM)] * 11,
        out_specs=pl.BlockSpec(memory_space=pltpu.VMEM),
        scratch_shapes=[
            pltpu.SMEM((16,), jnp.int32),
            pltpu.SMEM((128,), jnp.int32),
            pltpu.SMEM((128,), jnp.int32),
            pltpu.VMEM((1, 128), jnp.int32),
            pltpu.VMEM((1, 128), jnp.int32),
            pltpu.VMEM((ROWS, 2 * FL), BF16),
            pltpu.VMEM((CAP, 512), F32),
            pltpu.VMEM((5, 8, 128), F32),
            pltpu.VMEM((384, 128), F32),
            pltpu.VMEM((384, 128), BF16),
            pltpu.VMEM((512, 256), BF16),
            pltpu.VMEM((16, ROWS, 1024), BF16),
            pltpu.VMEM((576, 128), F32),
            pltpu.VMEM((128, 128), jnp.int32),
            pltpu.VMEM((2, BLOCKS + 1, 128, 128), F32),
            pltpu.VMEM((2, BLOCKS, 8, 512), F32),
            pltpu.VMEM((512, 128), BF16),
            pltpu.VMEM((512, 256), BF16),
            pltpu.VMEM((SPOTS, 512), BF16),
            pltpu.VMEM((NF, 16, 128), BF16),
            pltpu.VMEM((NF, 4, 16, 128), BF16),
            pltpu.VMEM((NF, 4, 16, 128), BF16),
            pltpu.VMEM((2, NF, 2, 16, 128), BF16),
            pltpu.VMEM((2, NF, 2, 16, 128), BF16),
            pltpu.VMEM((NF, 2, 128), BF16),
            pltpu.VMEM((NS, NF, 2, 128), BF16),
            pltpu.VMEM((128, 256), BF16),
            pltpu.VMEM((NF, 16, 128), BF16),
            pltpu.VMEM((NF, 16, 128), BF16),
            pltpu.VMEM((256, 512), BF16),
            pltpu.VMEM((576, 128), F32),
            dma((10,)), dma, pltpu.SemaphoreType.REGULAR((NS,)), dma, dma, dma((2,)), dma((2,)), dma, dma, dma, dma,
        ],
        compiler_params=pltpu.CompilerParams(collective_id=0, has_side_effects=True, vmem_limit_bytes=16*1024*1024),
        name="round_trip",
    )(
        *[
            pltpu.with_memory_space_constraint(a, pltpu.HBM)
            for a in (
                facet_offset, subgrid_offset, screen_index, subgrid_offset.reshape(1, -1), owner.reshape(1, -1),
                strips[0], grid_weight, twists, narrow, wide, screens,
            )
        ]
    )
    return result[None]


def solution(mesh):
    in_specs = (P("facet", "sub", None), P(), P(), P(), P(), P(), P(("facet", "sub"), None))
    out_specs = P("facet", "sub", None)
    return jax.shard_map(local, mesh=mesh, in_specs=in_specs, out_specs=out_specs, check_vma=False)
```

```python
import math

import jax
import jax.numpy as jnp
import numpy as np
from jax import lax
from jax.experimental import pallas as pl
from jax.experimental.pallas import tpu as pltpu
from jax.sharding import PartitionSpec as P

FL = 4096
CAP = 4
NF = 16
NS = 8
ROWS = 8
MINE = 8
BLOCKS = 9
SPOTS = BLOCKS * 16
MESH = pl.DeviceIdType.MESH
F32 = jnp.float32
BF16 = jnp.bfloat16


def split_halves(table):
    high = table.astype(np.float32).astype(jnp.bfloat16)
    low = (table - high.astype(np.float64)).astype(np.float32).astype(jnp.bfloat16)
    return high, low


def make_tables():
    k = np.arange(64)
    u = np.arange(32)
    b = np.arange(128)
    tau = 2.0 * np.pi
    first = tau * ((2 * k[:, None] * u[None, :]) % 64) / 64
    twist = tau * ((k[:, None] * b[None, :]) % FL) / FL
    last = tau * ((k[:, None] * b[None, :]) % 64) / 64
    scale = 1.0 / math.sqrt(FL)
    c, s = np.cos(first) * scale, np.sin(first) * scale
    ahead = np.concatenate(split_halves(np.block([[c, s], [-s, c]])), axis=1)
    cl, sl = np.cos(last), np.sin(last)
    frow = np.concatenate(split_halves(np.block([[cl, sl], [-sl, cl]])), axis=0)
    cb, sb = cl[:, :64].T, sl[:, :64].T
    brow = np.concatenate(split_halves(np.block([[cb, -sb], [sb, cb]])), axis=0)
    back = np.zeros((2, 2, 32, 2, 2, 64))
    for r in range(2):
        back[r, 0, :, 0, r], back[r, 0, :, 1, r] = c.T, -s.T
        back[r, 1, :, 0, r], back[r, 1, :, 1, r] = s.T, c.T
    back = np.concatenate(split_halves(back.reshape(128, 256)), axis=0)
    ct, st = np.cos(twist), np.sin(twist)
    twists = np.concatenate([ct, st, np.tile(ct.T, (1, 2)), np.tile(st.T, (1, 2))], axis=0).astype(np.float32)
    narrow = np.concatenate([ahead, brow], axis=0)
    wide = np.concatenate([frow, back], axis=0)
    return twists, narrow, wide


def mm(a, b):
    return jnp.dot(a, b, preferred_element_type=F32)


def mm_nt(a, b):
    return lax.dot_general(a, b, (((1,), (1,)), ((), ())), preferred_element_type=F32)


def halves(x):
    high = x.astype(BF16)
    return high, (x - high.astype(F32)).astype(BF16)


def iota(shape, dim):
    return lax.broadcasted_iota(jnp.int32, shape, dim)


def rows_of(*parts):
    return jnp.concatenate(parts, axis=0)


def lanes_of(*parts):
    return jnp.concatenate(parts, axis=1)


def both_parts(column):
    shaped = column.reshape(NF, MINE, 128)
    return jnp.concatenate([shaped, shaped], axis=1).reshape(256, 128)


def ones_where(mask):
    return jnp.where(mask, 1.0, 0.0).astype(BF16)


def kernel(
    fo_in, so_in, si_in, so_v_in, ow_v_in, strips_in, gw_in, twists_in, narrow_in, wide_in, screens, out,
    fo, so, si, so_v, ow_v, strips, gw, gwq, twists, narrow, wide, scr,
    xs, col, qsc, qfin, picks, spread, gather, low_mask, sbuf, rbuf, esend, ebuf,
    wout, wgot, chosen, wlow, whigh, tback, oscr,
    in_sem, scr_sem, known, s1, r1, s2, r2, sw1, rw1, sw2, rw2,
):
    f = lax.axis_index("facet")
    s = lax.axis_index("sub")
    fx, fy = f // 4, f % 4
    steps = [(dx, dy) for dx in range(4) for dy in range(4) if (dx, dy) != (0, 0)]
    steps.sort(key=lambda d: -(min(d[0], 4 - d[0]) + min(d[1], 4 - d[1])))
    peers = [((fx + dx) % 4) * 4 + (fy + dy) % 4 for dx, dy in steps]

    fetch = [
        pltpu.make_async_copy(a, b, in_sem.at[n])
        for n, (a, b) in enumerate(
            [
                (strips_in, strips), (so_v_in, so_v), (ow_v_in, ow_v), (narrow_in, narrow), (twists_in, twists),
                (wide_in, wide), (gw_in, gw), (fo_in, fo), (so_in, so), (si_in, si),
            ]
        )
    ]
    barrier = pltpu.get_barrier_semaphore()
    for p in peers:
        pl.semaphore_signal(barrier, inc=1, device_id=(p, s), device_id_type=MESH)
    for c in fetch:
        c.start()

    def greet(t, carry):
        pl.semaphore_signal(barrier, inc=1, device_id=(f, t), device_id_type=MESH)
        return carry

    lax.fori_loop(s + 1, NS, greet, 0)
    screen_copy = pltpu.make_async_copy(screens.at[:, pl.ds(pl.multiple_of(s * ROWS, ROWS), ROWS), :], scr, scr_sem)
    screen_copy.start()

    lane = iota((128, 128), 1)
    lane4 = iota((256, 128), 1)
    part4 = (iota((256, 128), 0) >> 3) & 1
    for c in fetch:
        c.wait()

    so_col = jnp.transpose(jnp.broadcast_to(so_v[...], (128, 128)))
    ow_row = jnp.broadcast_to(ow_v[...], (128, 128))
    ow_col = jnp.transpose(ow_row)
    col[...] = so_col
    start_col = (so_col + fo[f]) & (FL - 1)
    q4 = both_parts(start_col >> 6)
    take_low = (lane4 & 63) >= both_parts(start_col & 63)
    picks[:256] = ones_where(lane4 == q4 + 64 * part4)
    picks[256:] = ones_where(lane4 == ((q4 + 1) & 63) + 64 * part4)

    tf_high = mm(picks[...], wide[:128]).astype(BF16)
    tf_low = mm(picks[...], wide[128:256]).astype(BF16)
    for v in range(64):
        xs[pl.ds(8 * v, 8), :] = strips[:, 128 * v : 128 * v + 128].astype(F32)
    tc = lanes_of(twists[:64], twists[:64])
    ts = lanes_of(twists[64:128], twists[64:128])

    for h in range(2):
        columns = []
        for pair in (2 * h, 2 * h + 1):
            x = lanes_of(xs[pl.ds(2 * pair, 64, stride=8), :], xs[pl.ds(2 * pair + 1, 64, stride=8), :]).astype(BF16)
            a = mm(narrow[:128], rows_of(x, x))
            re, im = a[:64], a[64:]
            b_re = re * tc + im * ts
            b_im = im * tc - re * ts
            columns += [lanes_of(b_re[:, :128], b_im[:, :128]), lanes_of(b_re[:, 128:], b_im[:, 128:])]
        b_high, b_low = halves(rows_of(*columns))
        g = mm_nt(tf_high, b_high) + mm_nt(tf_low, b_high) + mm_nt(tf_high, b_low)
        for n in range(2):
            block = slice(128 * n, 128 * n + 128)
            piece = jnp.where(take_low, g[:256, block], g[256:, block]).astype(BF16)
            sbuf[:, 2 * h + n] = piece.reshape(NF, 16, 128)
    rbuf[pl.ds(f, 1)] = sbuf[pl.ds(f, 1)]

    lane_cap = iota((8, 128), 1)
    gwq[...] = jnp.zeros((5, 8, 128), F32)
    for q in range(4):
        gwq[q, pl.ds(0, CAP), :] = gw[:, 128 * q : 128 * q + 128]
    for n in range(NF):
        shift = fo[n] & 127
        block = fo[n] >> 7
        turn = (128 - shift) & 127
        window = jnp.where(
            lane_cap < 128 - shift, pltpu.roll(gwq[block], turn, 1), pltpu.roll(gwq[block + 1], turn, 1)
        )
        beside = pltpu.roll(pltpu.roll(window, 6, 0), 64, 1)
        wout[n] = jnp.where(lane_cap < 64, window, beside)[:2].astype(BF16)
    wgot[pl.ds(s, 1), pl.ds(f, 1)] = wout[pl.ds(f, 1)][None]

    pl.semaphore_wait(barrier, NF - 1 + s)

    def remote(src, dst, send, recv, to):
        return pltpu.make_async_remote_copy(
            src_ref=src, dst_ref=dst, send_sem=send, recv_sem=recv, device_id=to, device_id_type=MESH
        )

    def everything(buffer, send, recv):
        return remote(buffer, buffer, send, recv, (peers[0], s))

    for p in peers:
        remote(wout.at[p], wgot.at[s, f], sw1, rw1, (p, s)).start()
    for p in peers:
        remote(sbuf.at[p], rbuf.at[f], s1, r1, (p, s)).start()

    def tell(t, carry):
        pl.semaphore_signal(known.at[s], inc=1, device_id=(f, t), device_id_type=MESH)
        return carry

    def hear(t, carry):
        pl.semaphore_wait(known.at[t], 1)
        return carry

    def weights_to(t, carry):
        remote(wgot.at[s], wgot.at[s], sw2, rw2, (f, t)).start()
        return carry

    lax.fori_loop(0, s, tell, 0)

    tback[...] = mm_nt(narrow[128:], picks[...]).astype(BF16)

    lane8 = iota((8, 128), 1)
    left = lane8 < 64
    base = pl.multiple_of(f * MINE, MINE)
    r8 = col[pl.ds(base, MINE), :] & 63
    zero = jnp.zeros((8, 128), F32)
    screen_copy.wait()
    for j in range(MINE):
        shift = so[base + j] & 63
        screen = scr[si[base + j]].astype(F32)
        for part in range(2):
            rolled = [
                pltpu.roll(screen[:, 512 * part + 128 * v : 512 * part + 128 * v + 128], shift, 1) for v in range(4)
            ]
            rolled = [zero] + rolled + [zero]
            for v in range(5):
                piece = jnp.where(lane8 >= shift, rolled[v + 1], rolled[v])
                other = pltpu.roll(piece, 64, 1)
                qsc[part, 2 * v, pl.ds(j, ROWS, stride=MINE), :] = jnp.where(left, piece, other)
                if 2 * v + 1 < BLOCKS:
                    qsc[part, 2 * v + 1, pl.ds(j, ROWS, stride=MINE), :] = jnp.where(left, other, piece)
    for part in range(2):
        for b in range(BLOCKS):
            for pair in range(4):
                at = 16 * pair
                qfin[part, b, :, pl.ds(128 * pair, 128)] = jnp.where(
                    left, qsc[part, b, pl.ds(at, 8), :], qsc[part, b, pl.ds(at + 8, 8), :]
                )

    lane256 = iota((8, 256), 1)
    own = iota((8, 256), 0)
    r8w = lanes_of(r8, r8)
    for n in range(NF):
        first = ((r8w + fo[n]) >> 6) * 16 + own
        for late in range(2):
            spot = first + 16 * late
            at = 256 * late + 16 * n
            spread[pl.ds(at, 16), :] = rows_of(
                jnp.where(lane256 == spot, 1.0, 0.0), jnp.where(lane256 == spot + 8, 1.0, 0.0)
            ).astype(BF16)
        mask = jnp.where((lane8 & 63) >= ((r8 + fo[n]) & 63), 1.0, 0.0)
        low_mask[n] = rows_of(mask, mask).astype(BF16)
    unit = ones_where(iota((SPOTS, 256), 0) == iota((SPOTS, 256), 1))
    gather[...] = mm_nt(unit, spread[...]).astype(BF16)

    everything(wgot.at[0, pl.ds(0, NF - 1)], sw1, rw1).wait_recv()
    lax.fori_loop(0, s, weights_to, 0)

    everything(rbuf.at[pl.ds(0, NF - 1)], s1, r1).wait_recv()

    nothing = jnp.zeros((256 - SPOTS, 256), BF16)
    for h in range(2):
        low, high = [], []
        for pair in (2 * h, 2 * h + 1):
            c = rbuf[:, pair]
            c_low = c * low_mask[...]
            low.append(c_low.reshape(256, 128))
            high.append((c - c_low).reshape(256, 128))
        sums = mm(gather[...], rows_of(lanes_of(*low), lanes_of(*high)))
        done = []
        lanes = pl.ds(256 * h, 256)
        for b in range(BLOCKS):
            re, im = sums[16 * b : 16 * b + 8], sums[16 * b + 8 : 16 * b + 16]
            cs, sn = qfin[0, b, :, lanes], qfin[1, b, :, lanes]
            done += [re * cs - im * sn, re * sn + im * cs]
        both = mm(spread[...], rows_of(rows_of(*done).astype(BF16), nothing))
        keep = low_mask[...].reshape(256, 128) > 0
        for n in range(2):
            block = slice(128 * n, 128 * n + 128)
            piece = jnp.where(keep, both[:256, block], both[256:, block]).astype(BF16)
            esend[h, :, n] = piece.reshape(NF, 16, 128)
        for p in peers:
            remote(esend.at[h, p], ebuf.at[h, f], s2.at[h], r2.at[h], (p, s)).start()
    ebuf[:, pl.ds(f, 1)] = esend[:, pl.ds(f, 1)]

    lax.fori_loop(s + 1, NS, hear, 0)
    lax.fori_loop(s + 1, NS, weights_to, 0)

    ow_row = jnp.broadcast_to(ow_v[...], (128, 128))
    ow_col = jnp.transpose(ow_row)
    earlier = jnp.where((ow_row == ow_col) & (lane < iota((128, 128), 0)), 1.0, 0.0)
    slot = jnp.sum(earlier, axis=1, keepdims=True).astype(jnp.int32)
    weight_row = ow_col * CAP + slot
    spot = 32 * ((weight_row >> 2) & 7) + 2 * (weight_row >> 5) + (weight_row & 1)
    chosen[...] = ones_where(iota((128, 256), 1) == lanes_of(spot, spot))
    upper = (weight_row & 2) == 2
    r_col = (col[...] + fo[f]) & 63
    everything(wgot.at[pl.ds(0, NS - 1)], sw2, rw2).wait_recv()
    rows = mm(chosen[...], wgot[...].reshape(256, 128))
    weight = jnp.where((lane < 64) != upper, rows, pltpu.roll(rows, 64, 1))
    for bit in range(6):
        amount = 1 << bit
        weight = jnp.where((r_col & amount) != 0, pltpu.roll(weight, amount, 1), weight)
    weight4 = both_parts(weight)
    first4 = (lane4 & 63) >= both_parts(r_col)
    wlow[...] = jnp.where(first4, weight4, 0.0).astype(BF16).reshape(NF, 16, 128)
    whigh[...] = jnp.where(first4, 0.0, weight4).astype(BF16).reshape(NF, 16, 128)

    for h in range(2):
        everything(ebuf.at[h, pl.ds(0, NF - 1)], s2.at[h], r2.at[h]).wait_recv()
    for h in range(2):
        low, high = [], []
        for n in range(2):
            e = ebuf[h, :, n]
            low.append((e * wlow[...]).reshape(256, 128))
            high.append((e * whigh[...]).reshape(256, 128))
        d = mm(tback[...], rows_of(lanes_of(*low), lanes_of(*high)))
        d = d[:128] + d[128:]
        re, im = d[:64], d[64:]
        d_re, d_im = [], []
        for turn in range(2):
            at = pl.ds(128 + 64 * turn, 64)
            cs = lanes_of(twists[at, :], twists[at, :])
            at = pl.ds(256 + 64 * turn, 64)
            sn = lanes_of(twists[at, :], twists[at, :])
            d_re.append(re * cs - im * sn)
            d_im.append(re * sn + im * cs)
        d_re, d_im = rows_of(*d_re), rows_of(*d_im)
        d_high, d_low = halves(
            rows_of(lanes_of(d_re[:, :128], d_im[:, :128]), lanes_of(d_re[:, 128:], d_im[:, 128:]))
        )
        o = mm_nt(wide[256:], d_high)
        o = o[:128] + o[128:] + mm_nt(wide[256:384], d_low)
        for n in range(2):
            for r in range(2):
                oscr[pl.ds(4 * h + 2 * n + r, 64, stride=8), :] = o[64 * r : 64 * r + 64, 128 * n : 128 * n + 128]
    for v in range(64):
        out[:, 128 * v : 128 * v + 128] = oscr[pl.ds(8 * v, 8), :]

    everything(sbuf.at[pl.ds(0, NF - 1)], s1, r1).wait_send()
    everything(wout.at[pl.ds(0, NF - 1)], sw1, rw1).wait_send()
    everything(wgot.at[pl.ds(0, NS - 1)], sw2, rw2).wait_send()
    for h in range(2):
        everything(esend.at[h, pl.ds(0, NF - 1)], s2.at[h], r2.at[h]).wait_send()


def local(strips, facet_offset, subgrid_offset, owner, screen_index, screens, grid_weight):
    twists, narrow, wide = [jnp.asarray(t) for t in make_tables()]
    dma = pltpu.SemaphoreType.DMA
    result = pl.pallas_call(
        kernel,
        out_shape=jax.ShapeDtypeStruct((ROWS, 2 * FL), F32),
        in_specs=[pl.BlockSpec(memory_space=pltpu.HBM)] * 11,
        out_specs=pl.BlockSpec(memory_space=pltpu.VMEM),
        scratch_shapes=[
            pltpu.SMEM((16,), jnp.int32),
            pltpu.SMEM((128,), jnp.int32),
            pltpu.SMEM((128,), jnp.int32),
            pltpu.VMEM((1, 128), jnp.int32),
            pltpu.VMEM((1, 128), jnp.int32),
            pltpu.VMEM((ROWS, 2 * FL), BF16),
            pltpu.VMEM((CAP, 512), F32),
            pltpu.VMEM((5, 8, 128), F32),
            pltpu.VMEM((384, 128), F32),
            pltpu.VMEM((384, 128), BF16),
            pltpu.VMEM((512, 256), BF16),
            pltpu.VMEM((16, ROWS, 1024), BF16),
            pltpu.VMEM((576, 128), F32),
            pltpu.VMEM((128, 128), jnp.int32),
            pltpu.VMEM((2, BLOCKS + 1, 128, 128), F32),
            pltpu.VMEM((2, BLOCKS, 8, 512), F32),
            pltpu.VMEM((512, 128), BF16),
            pltpu.VMEM((512, 256), BF16),
            pltpu.VMEM((SPOTS, 512), BF16),
            pltpu.VMEM((NF, 16, 128), BF16),
            pltpu.VMEM((NF, 4, 16, 128), BF16),
            pltpu.VMEM((NF, 4, 16, 128), BF16),
            pltpu.VMEM((2, NF, 2, 16, 128), BF16),
            pltpu.VMEM((2, NF, 2, 16, 128), BF16),
            pltpu.VMEM((NF, 2, 128), BF16),
            pltpu.VMEM((NS, NF, 2, 128), BF16),
            pltpu.VMEM((128, 256), BF16),
            pltpu.VMEM((NF, 16, 128), BF16),
            pltpu.VMEM((NF, 16, 128), BF16),
            pltpu.VMEM((256, 512), BF16),
            pltpu.VMEM((576, 128), F32),
            dma((10,)), dma, pltpu.SemaphoreType.REGULAR((NS,)), dma, dma, dma((2,)), dma((2,)), dma, dma, dma, dma,
        ],
        compiler_params=pltpu.CompilerParams(collective_id=0, has_side_effects=True, vmem_limit_bytes=16*1024*1024),
        name="round_trip",
    )(
        *[
            pltpu.with_memory_space_constraint(a, pltpu.HBM)
            for a in (
                facet_offset, subgrid_offset, screen_index, subgrid_offset.reshape(1, -1), owner.reshape(1, -1),
                strips[0], grid_weight, twists, narrow, wide, screens,
            )
        ]
    )
    return result[None]


def solution(mesh):
    in_specs = (P("facet", "sub", None), P(), P(), P(), P(), P(), P(("facet", "sub"), None))
    out_specs = P("facet", "sub", None)
    return jax.shard_map(local, mesh=mesh, in_specs=in_specs, out_specs=out_specs, check_vma=False)
```

```python
import math

import jax
import jax.numpy as jnp
import numpy as np
from jax import lax
from jax.experimental import pallas as pl
from jax.experimental.pallas import tpu as pltpu
from jax.sharding import PartitionSpec as P

FL = 4096
CAP = 4
NF = 16
NS = 8
ROWS = 8
MINE = 8
BLOCKS = 9
SPOTS = BLOCKS * 16
MESH = pl.DeviceIdType.MESH
F32 = jnp.float32
BF16 = jnp.bfloat16


def split_halves(table):
    high = table.astype(np.float32).astype(jnp.bfloat16)
    low = (table - high.astype(np.float64)).astype(np.float32).astype(jnp.bfloat16)
    return high, low


def make_tables():
    k = np.arange(64)
    u = np.arange(32)
    b = np.arange(128)
    tau = 2.0 * np.pi
    first = tau * ((2 * k[:, None] * u[None, :]) % 64) / 64
    twist = tau * ((k[:, None] * b[None, :]) % FL) / FL
    last = tau * ((k[:, None] * b[None, :]) % 64) / 64
    scale = 1.0 / math.sqrt(FL)
    c, s = np.cos(first) * scale, np.sin(first) * scale
    ahead = np.concatenate(split_halves(np.block([[c, s], [-s, c]])), axis=1)
    cl, sl = np.cos(last), np.sin(last)
    frow = np.concatenate(split_halves(np.block([[cl, sl], [-sl, cl]])), axis=0)
    cb, sb = cl[:, :64].T, sl[:, :64].T
    brow = np.concatenate(split_halves(np.block([[cb, -sb], [sb, cb]])), axis=0)
    back = np.zeros((2, 2, 32, 2, 2, 64))
    for r in range(2):
        back[r, 0, :, 0, r], back[r, 0, :, 1, r] = c.T, -s.T
        back[r, 1, :, 0, r], back[r, 1, :, 1, r] = s.T, c.T
    back = np.concatenate(split_halves(back.reshape(128, 256)), axis=0)
    ct, st = np.cos(twist), np.sin(twist)
    twists = np.concatenate([ct, st, np.tile(ct.T, (1, 2)), np.tile(st.T, (1, 2))], axis=0).astype(np.float32)
    narrow = np.concatenate([ahead, brow], axis=0)
    wide = np.concatenate([frow, back], axis=0)
    return twists, narrow, wide


def mm(a, b):
    return jnp.dot(a, b, preferred_element_type=F32)


def mm_nt(a, b):
    return lax.dot_general(a, b, (((1,), (1,)), ((), ())), preferred_element_type=F32)


def halves(x):
    high = x.astype(BF16)
    return high, (x - high.astype(F32)).astype(BF16)


def iota(shape, dim):
    return lax.broadcasted_iota(jnp.int32, shape, dim)


def rows_of(*parts):
    return jnp.concatenate(parts, axis=0)


def lanes_of(*parts):
    return jnp.concatenate(parts, axis=1)


def both_parts(column):
    shaped = column.reshape(NF, MINE, 128)
    return jnp.concatenate([shaped, shaped], axis=1).reshape(256, 128)


def ones_where(mask):
    return jnp.where(mask, 1.0, 0.0).astype(BF16)


def kernel(
    fo_in, so_in, si_in, so_v_in, ow_v_in, strips_in, gw_in, twists_in, narrow_in, wide_in, screens, out,
    fo, so, si, so_v, ow_v, strips, gw, gwq, twists, narrow, wide, scr,
    xs, col, qsc, qfin, picks, spread, gather, low_mask, sbuf, rbuf, esend, ebuf,
    wout, wgot, chosen, wlow, whigh, tback, oscr,
    in_sem, scr_sem, known, s1, r1, s2, r2, sw1, rw1, sw2, rw2,
):
    f = lax.axis_index("facet")
    s = lax.axis_index("sub")
    fx, fy = f // 4, f % 4
    steps = [(dx, dy) for dx in range(4) for dy in range(4) if (dx, dy) != (0, 0)]
    steps.sort(key=lambda d: -(min(d[0], 4 - d[0]) + min(d[1], 4 - d[1])))
    peers = [((fx + dx) % 4) * 4 + (fy + dy) % 4 for dx, dy in steps]

    fetch = [
        pltpu.make_async_copy(a, b, in_sem.at[n])
        for n, (a, b) in enumerate(
            [
                (strips_in, strips), (so_v_in, so_v), (ow_v_in, ow_v), (narrow_in, narrow), (twists_in, twists),
                (wide_in, wide), (gw_in, gw), (fo_in, fo), (so_in, so), (si_in, si),
            ]
        )
    ]
    barrier = pltpu.get_barrier_semaphore()
    for p in peers:
        pl.semaphore_signal(barrier, inc=1, device_id=(p, s), device_id_type=MESH)
    for c in fetch:
        c.start()

    def greet(t, carry):
        pl.semaphore_signal(barrier, inc=1, device_id=(f, t), device_id_type=MESH)
        return carry

    lax.fori_loop(s + 1, NS, greet, 0)
    screen_copy = pltpu.make_async_copy(screens.at[:, pl.ds(pl.multiple_of(s * ROWS, ROWS), ROWS), :], scr, scr_sem)
    screen_copy.start()

    lane = iota((128, 128), 1)
    lane4 = iota((256, 128), 1)
    part4 = (iota((256, 128), 0) >> 3) & 1
    for c in fetch:
        c.wait()

    so_col = jnp.transpose(jnp.broadcast_to(so_v[...], (128, 128)))
    ow_row = jnp.broadcast_to(ow_v[...], (128, 128))
    ow_col = jnp.transpose(ow_row)
    col[...] = so_col
    start_col = (so_col + fo[f]) & (FL - 1)
    q4 = both_parts(start_col >> 6)
    take_low = (lane4 & 63) >= both_parts(start_col & 63)
    picks[:256] = ones_where(lane4 == q4 + 64 * part4)
    picks[256:] = ones_where(lane4 == ((q4 + 1) & 63) + 64 * part4)

    tf_high = mm(picks[...], wide[:128]).astype(BF16)
    tf_low = mm(picks[...], wide[128:256]).astype(BF16)
    for v in range(64):
        xs[pl.ds(8 * v, 8), :] = strips[:, 128 * v : 128 * v + 128].astype(F32)
    tc = lanes_of(twists[:64], twists[:64])
    ts = lanes_of(twists[64:128], twists[64:128])

    for h in range(2):
        columns = []
        for pair in (2 * h, 2 * h + 1):
            x = lanes_of(xs[pl.ds(2 * pair, 64, stride=8), :], xs[pl.ds(2 * pair + 1, 64, stride=8), :]).astype(BF16)
            a = mm(narrow[:128], rows_of(x, x))
            re, im = a[:64], a[64:]
            b_re = re * tc + im * ts
            b_im = im * tc - re * ts
            columns += [lanes_of(b_re[:, :128], b_im[:, :128]), lanes_of(b_re[:, 128:], b_im[:, 128:])]
        b_high, b_low = halves(rows_of(*columns))
        g = mm_nt(tf_high, b_high) + mm_nt(tf_low, b_high) + mm_nt(tf_high, b_low)
        for n in range(2):
            block = slice(128 * n, 128 * n + 128)
            piece = jnp.where(take_low, g[:256, block], g[256:, block]).astype(BF16)
            sbuf[:, 2 * h + n] = piece.reshape(NF, 16, 128)
    rbuf[pl.ds(f, 1)] = sbuf[pl.ds(f, 1)]

    lane_cap = iota((8, 128), 1)
    gwq[...] = jnp.zeros((5, 8, 128), F32)
    for q in range(4):
        gwq[q, pl.ds(0, CAP), :] = gw[:, 128 * q : 128 * q + 128]
    for n in range(NF):
        shift = fo[n] & 127
        block = fo[n] >> 7
        turn = (128 - shift) & 127
        window = jnp.where(
            lane_cap < 128 - shift, pltpu.roll(gwq[block], turn, 1), pltpu.roll(gwq[block + 1], turn, 1)
        )
        beside = pltpu.roll(pltpu.roll(window, 6, 0), 64, 1)
        wout[n] = jnp.where(lane_cap < 64, window, beside)[:2].astype(BF16)
    wgot[pl.ds(s, 1), pl.ds(f, 1)] = wout[pl.ds(f, 1)][None]

    pl.semaphore_wait(barrier, NF - 1 + s)

    def remote(src, dst, send, recv, to):
        return pltpu.make_async_remote_copy(
            src_ref=src, dst_ref=dst, send_sem=send, recv_sem=recv, device_id=to, device_id_type=MESH
        )

    def everything(buffer, send, recv):
        return remote(buffer, buffer, send, recv, (peers[0], s))

    for p in peers:
        remote(wout.at[p], wgot.at[s, f], sw1, rw1, (p, s)).start()
    for p in peers:
        remote(sbuf.at[p], rbuf.at[f], s1, r1, (p, s)).start()

    def tell(t, carry):
        pl.semaphore_signal(known.at[s], inc=1, device_id=(f, t), device_id_type=MESH)
        return carry

    def hear(t, carry):
        pl.semaphore_wait(known.at[t], 1)
        return carry

    def weights_to(t, carry):
        remote(wgot.at[s], wgot.at[s], sw2, rw2, (f, t)).start()
        return carry

    lax.fori_loop(0, s, tell, 0)

    tback[...] = mm_nt(narrow[128:], picks[...]).astype(BF16)

    lane8 = iota((8, 128), 1)
    left = lane8 < 64
    base = pl.multiple_of(f * MINE, MINE)
    r8 = col[pl.ds(base, MINE), :] & 63
    zero = jnp.zeros((8, 128), F32)
    screen_copy.wait()
    for j in range(MINE):
        shift = so[base + j] & 63
        screen = scr[si[base + j]].astype(F32)
        for part in range(2):
            rolled = [
                pltpu.roll(screen[:, 512 * part + 128 * v : 512 * part + 128 * v + 128], shift, 1) for v in range(4)
            ]
            rolled = [zero] + rolled + [zero]
            for v in range(5):
                piece = jnp.where(lane8 >= shift, rolled[v + 1], rolled[v])
                other = pltpu.roll(piece, 64, 1)
                qsc[part, 2 * v, pl.ds(j, ROWS, stride=MINE), :] = jnp.where(left, piece, other)
                if 2 * v + 1 < BLOCKS:
                    qsc[part, 2 * v + 1, pl.ds(j, ROWS, stride=MINE), :] = jnp.where(left, other, piece)
    for part in range(2):
        for b in range(BLOCKS):
            for pair in range(4):
                at = 16 * pair
                qfin[part, b, :, pl.ds(128 * pair, 128)] = jnp.where(
                    left, qsc[part, b, pl.ds(at, 8), :], qsc[part, b, pl.ds(at + 8, 8), :]
                )

    lane256 = iota((8, 256), 1)
    own = iota((8, 256), 0)
    r8w = lanes_of(r8, r8)
    for n in range(NF):
        first = ((r8w + fo[n]) >> 6) * 16 + own
        for late in range(2):
            spot = first + 16 * late
            at = 256 * late + 16 * n
            spread[pl.ds(at, 16), :] = rows_of(
                jnp.where(lane256 == spot, 1.0, 0.0), jnp.where(lane256 == spot + 8, 1.0, 0.0)
            ).astype(BF16)
        mask = jnp.where((lane8 & 63) >= ((r8 + fo[n]) & 63), 1.0, 0.0)
        low_mask[n] = rows_of(mask, mask).astype(BF16)
    unit = ones_where(iota((SPOTS, 256), 0) == iota((SPOTS, 256), 1))
    gather[...] = mm_nt(unit, spread[...]).astype(BF16)

    everything(wgot.at[0, pl.ds(0, NF - 1)], sw1, rw1).wait_recv()
    lax.fori_loop(0, s, weights_to, 0)

    everything(rbuf.at[pl.ds(0, NF - 1)], s1, r1).wait_recv()

    nothing = jnp.zeros((256 - SPOTS, 256), BF16)
    for h in range(2):
        low, high = [], []
        for pair in (2 * h, 2 * h + 1):
            c = rbuf[:, pair]
            c_low = c * low_mask[...]
            low.append(c_low.reshape(256, 128))
            high.append((c - c_low).reshape(256, 128))
        sums = mm(gather[...], rows_of(lanes_of(*low), lanes_of(*high)))
        done = []
        lanes = pl.ds(256 * h, 256)
        for b in range(BLOCKS):
            re, im = sums[16 * b : 16 * b + 8], sums[16 * b + 8 : 16 * b + 16]
            cs, sn = qfin[0, b, :, lanes], qfin[1, b, :, lanes]
            done += [re * cs - im * sn, re * sn + im * cs]
        both = mm(spread[...], rows_of(rows_of(*done).astype(BF16), nothing))
        keep = low_mask[...].reshape(256, 128) > 0
        for n in range(2):
            block = slice(128 * n, 128 * n + 128)
            piece = jnp.where(keep, both[:256, block], both[256:, block]).astype(BF16)
            esend[h, :, n] = piece.reshape(NF, 16, 128)
        if h == 1:
            for p in peers:
                remote(esend.at[:, p], ebuf.at[:, f], s2, r2, (p, s)).start()
    ebuf[:, pl.ds(f, 1)] = esend[:, pl.ds(f, 1)]

    lax.fori_loop(s + 1, NS, hear, 0)
    lax.fori_loop(s + 1, NS, weights_to, 0)

    ow_row = jnp.broadcast_to(ow_v[...], (128, 128))
    ow_col = jnp.transpose(ow_row)
    earlier = jnp.where((ow_row == ow_col) & (lane < iota((128, 128), 0)), 1.0, 0.0)
    slot = jnp.sum(earlier, axis=1, keepdims=True).astype(jnp.int32)
    weight_row = ow_col * CAP + slot
    spot = 32 * ((weight_row >> 2) & 7) + 2 * (weight_row >> 5) + (weight_row & 1)
    chosen[...] = ones_where(iota((128, 256), 1) == lanes_of(spot, spot))
    upper = (weight_row & 2) == 2
    r_col = (col[...] + fo[f]) & 63
    everything(wgot.at[pl.ds(0, NS - 1)], sw2, rw2).wait_recv()
    rows = mm(chosen[...], wgot[...].reshape(256, 128))
    weight = jnp.where((lane < 64) != upper, rows, pltpu.roll(rows, 64, 1))
    for bit in range(6):
        amount = 1 << bit
        weight = jnp.where((r_col & amount) != 0, pltpu.roll(weight, amount, 1), weight)
    weight4 = both_parts(weight)
    first4 = (lane4 & 63) >= both_parts(r_col)
    wlow[...] = jnp.where(first4, weight4, 0.0).astype(BF16).reshape(NF, 16, 128)
    whigh[...] = jnp.where(first4, 0.0, weight4).astype(BF16).reshape(NF, 16, 128)

    everything(ebuf.at[:, pl.ds(0, NF - 1)], s2, r2).wait_recv()
    for h in range(2):
        low, high = [], []
        for n in range(2):
            e = ebuf[h, :, n]
            low.append((e * wlow[...]).reshape(256, 128))
            high.append((e * whigh[...]).reshape(256, 128))
        d = mm(tback[...], rows_of(lanes_of(*low), lanes_of(*high)))
        d = d[:128] + d[128:]
        re, im = d[:64], d[64:]
        d_re, d_im = [], []
        for turn in range(2):
            at = pl.ds(128 + 64 * turn, 64)
            cs = lanes_of(twists[at, :], twists[at, :])
            at = pl.ds(256 + 64 * turn, 64)
            sn = lanes_of(twists[at, :], twists[at, :])
            d_re.append(re * cs - im * sn)
            d_im.append(re * sn + im * cs)
        d_re, d_im = rows_of(*d_re), rows_of(*d_im)
        d_high, d_low = halves(
            rows_of(lanes_of(d_re[:, :128], d_im[:, :128]), lanes_of(d_re[:, 128:], d_im[:, 128:]))
        )
        o = mm_nt(wide[256:], d_high)
        o = o[:128] + o[128:] + mm_nt(wide[256:384], d_low)
        for n in range(2):
            for r in range(2):
                oscr[pl.ds(4 * h + 2 * n + r, 64, stride=8), :] = o[64 * r : 64 * r + 64, 128 * n : 128 * n + 128]
    for v in range(64):
        out[:, 128 * v : 128 * v + 128] = oscr[pl.ds(8 * v, 8), :]

    everything(sbuf.at[pl.ds(0, NF - 1)], s1, r1).wait_send()
    everything(wout.at[pl.ds(0, NF - 1)], sw1, rw1).wait_send()
    everything(wgot.at[pl.ds(0, NS - 1)], sw2, rw2).wait_send()
    everything(esend.at[:, pl.ds(0, NF - 1)], s2, r2).wait_send()


def local(strips, facet_offset, subgrid_offset, owner, screen_index, screens, grid_weight):
    twists, narrow, wide = [jnp.asarray(t) for t in make_tables()]
    dma = pltpu.SemaphoreType.DMA
    result = pl.pallas_call(
        kernel,
        out_shape=jax.ShapeDtypeStruct((ROWS, 2 * FL), F32),
        in_specs=[pl.BlockSpec(memory_space=pltpu.HBM)] * 11,
        out_specs=pl.BlockSpec(memory_space=pltpu.VMEM),
        scratch_shapes=[
            pltpu.SMEM((16,), jnp.int32),
            pltpu.SMEM((128,), jnp.int32),
            pltpu.SMEM((128,), jnp.int32),
            pltpu.VMEM((1, 128), jnp.int32),
            pltpu.VMEM((1, 128), jnp.int32),
            pltpu.VMEM((ROWS, 2 * FL), BF16),
            pltpu.VMEM((CAP, 512), F32),
            pltpu.VMEM((5, 8, 128), F32),
            pltpu.VMEM((384, 128), F32),
            pltpu.VMEM((384, 128), BF16),
            pltpu.VMEM((512, 256), BF16),
            pltpu.VMEM((16, ROWS, 1024), BF16),
            pltpu.VMEM((576, 128), F32),
            pltpu.VMEM((128, 128), jnp.int32),
            pltpu.VMEM((2, BLOCKS + 1, 128, 128), F32),
            pltpu.VMEM((2, BLOCKS, 8, 512), F32),
            pltpu.VMEM((512, 128), BF16),
            pltpu.VMEM((512, 256), BF16),
            pltpu.VMEM((SPOTS, 512), BF16),
            pltpu.VMEM((NF, 16, 128), BF16),
            pltpu.VMEM((NF, 4, 16, 128), BF16),
            pltpu.VMEM((NF, 4, 16, 128), BF16),
            pltpu.VMEM((2, NF, 2, 16, 128), BF16),
            pltpu.VMEM((2, NF, 2, 16, 128), BF16),
            pltpu.VMEM((NF, 2, 128), BF16),
            pltpu.VMEM((NS, NF, 2, 128), BF16),
            pltpu.VMEM((128, 256), BF16),
            pltpu.VMEM((NF, 16, 128), BF16),
            pltpu.VMEM((NF, 16, 128), BF16),
            pltpu.VMEM((256, 512), BF16),
            pltpu.VMEM((576, 128), F32),
            dma((10,)), dma, pltpu.SemaphoreType.REGULAR((NS,)), dma, dma, dma, dma, dma, dma, dma, dma,
        ],
        compiler_params=pltpu.CompilerParams(collective_id=0, has_side_effects=True, vmem_limit_bytes=16*1024*1024),
        name="round_trip",
    )(
        *[
            pltpu.with_memory_space_constraint(a, pltpu.HBM)
            for a in (
                facet_offset, subgrid_offset, screen_index, subgrid_offset.reshape(1, -1), owner.reshape(1, -1),
                strips[0], grid_weight, twists, narrow, wide, screens,
            )
        ]
    )
    return result[None]


def solution(mesh):
    in_specs = (P("facet", "sub", None), P(), P(), P(), P(), P(), P(("facet", "sub"), None))
    out_specs = P("facet", "sub", None)
    return jax.shard_map(local, mesh=mesh, in_specs=in_specs, out_specs=out_specs, check_vma=False)
```

```python
import math

import jax
import jax.numpy as jnp
import numpy as np
from jax import lax
from jax.experimental import pallas as pl
from jax.experimental.pallas import tpu as pltpu
from jax.sharding import PartitionSpec as P

FL = 4096
CAP = 4
NF = 16
NS = 8
ROWS = 8
MINE = 8
BLOCKS = 9
SPOTS = BLOCKS * 16
MESH = pl.DeviceIdType.MESH
F32 = jnp.float32
BF16 = jnp.bfloat16


def split_halves(table):
    high = table.astype(np.float32).astype(jnp.bfloat16)
    low = (table - high.astype(np.float64)).astype(np.float32).astype(jnp.bfloat16)
    return high, low


def make_tables():
    k = np.arange(64)
    u = np.arange(32)
    b = np.arange(128)
    tau = 2.0 * np.pi
    first = tau * ((2 * k[:, None] * u[None, :]) % 64) / 64
    twist = tau * ((k[:, None] * b[None, :]) % FL) / FL
    last = tau * ((k[:, None] * b[None, :]) % 64) / 64
    scale = 1.0 / math.sqrt(FL)
    c, s = np.cos(first) * scale, np.sin(first) * scale
    ahead = np.concatenate(split_halves(np.block([[c, s], [-s, c]])), axis=1)
    cl, sl = np.cos(last), np.sin(last)
    frow = np.concatenate(split_halves(np.block([[cl, sl], [-sl, cl]])), axis=0)
    cb, sb = cl[:, :64].T, sl[:, :64].T
    brow = np.concatenate(split_halves(np.block([[cb, -sb], [sb, cb]])), axis=0)
    back = np.zeros((2, 2, 32, 2, 2, 64))
    for r in range(2):
        back[r, 0, :, 0, r], back[r, 0, :, 1, r] = c.T, -s.T
        back[r, 1, :, 0, r], back[r, 1, :, 1, r] = s.T, c.T
    back = np.concatenate(split_halves(back.reshape(128, 256)), axis=0)
    ct, st = np.cos(twist), np.sin(twist)
    twists = np.concatenate([ct, st, np.tile(ct.T, (1, 2)), np.tile(st.T, (1, 2))], axis=0).astype(np.float32)
    narrow = np.concatenate([ahead, brow], axis=0)
    wide = np.concatenate([frow, back], axis=0)
    return twists, narrow, wide


def mm(a, b):
    return jnp.dot(a, b, preferred_element_type=F32)


def mm_nt(a, b):
    return lax.dot_general(a, b, (((1,), (1,)), ((), ())), preferred_element_type=F32)


def halves(x):
    high = x.astype(BF16)
    return high, (x - high.astype(F32)).astype(BF16)


def iota(shape, dim):
    return lax.broadcasted_iota(jnp.int32, shape, dim)


def rows_of(*parts):
    return jnp.concatenate(parts, axis=0)


def lanes_of(*parts):
    return jnp.concatenate(parts, axis=1)


def both_parts(column):
    shaped = column.reshape(NF, MINE, 128)
    return jnp.concatenate([shaped, shaped], axis=1).reshape(256, 128)


def ones_where(mask):
    return jnp.where(mask, 1.0, 0.0).astype(BF16)


def kernel(
    fo_in, so_in, si_in, so_v_in, ow_v_in, strips_in, gw_in, twists_in, narrow_in, wide_in, screens, out,
    fo, so, si, so_v, ow_v, strips, gw, gwq, twists, narrow, wide, scr,
    xs, col, qsc, qfin, picks, spread, gather, low_mask, sbuf, rbuf, esend, ebuf,
    wout, wgot, chosen, wlow, whigh, tback,
    in_sem, scr_sem, known, s1, r1, s2, r2, sw1, rw1, sw2, rw2,
):
    f = lax.axis_index("facet")
    s = lax.axis_index("sub")
    fx, fy = f // 4, f % 4
    steps = [(dx, dy) for dx in range(4) for dy in range(4) if (dx, dy) != (0, 0)]
    steps.sort(key=lambda d: -(min(d[0], 4 - d[0]) + min(d[1], 4 - d[1])))
    peers = [((fx + dx) % 4) * 4 + (fy + dy) % 4 for dx, dy in steps]

    fetch = [
        pltpu.make_async_copy(a, b, in_sem.at[n])
        for n, (a, b) in enumerate(
            [
                (strips_in, strips), (so_v_in, so_v), (ow_v_in, ow_v), (narrow_in, narrow), (twists_in, twists),
                (wide_in, wide), (gw_in, gw), (fo_in, fo), (so_in, so), (si_in, si),
            ]
        )
    ]
    barrier = pltpu.get_barrier_semaphore()
    for p in peers:
        pl.semaphore_signal(barrier, inc=1, device_id=(p, s), device_id_type=MESH)
    for c in fetch:
        c.start()

    def greet(t, carry):
        pl.semaphore_signal(barrier, inc=1, device_id=(f, t), device_id_type=MESH)
        return carry

    lax.fori_loop(s + 1, NS, greet, 0)
    screen_copy = pltpu.make_async_copy(screens.at[:, pl.ds(pl.multiple_of(s * ROWS, ROWS), ROWS), :], scr, scr_sem)
    screen_copy.start()

    lane = iota((128, 128), 1)
    lane4 = iota((256, 128), 1)
    part4 = (iota((256, 128), 0) >> 3) & 1
    for c in fetch:
        c.wait()

    so_col = jnp.transpose(jnp.broadcast_to(so_v[...], (128, 128)))
    ow_row = jnp.broadcast_to(ow_v[...], (128, 128))
    ow_col = jnp.transpose(ow_row)
    col[...] = so_col
    start_col = (so_col + fo[f]) & (FL - 1)
    q4 = both_parts(start_col >> 6)
    take_low = (lane4 & 63) >= both_parts(start_col & 63)
    picks[:256] = ones_where(lane4 == q4 + 64 * part4)
    picks[256:] = ones_where(lane4 == ((q4 + 1) & 63) + 64 * part4)

    tf_high = mm(picks[...], wide[:128]).astype(BF16)
    tf_low = mm(picks[...], wide[128:256]).astype(BF16)
    for v in range(64):
        xs[pl.ds(8 * v, 8), :] = strips[:, 128 * v : 128 * v + 128].astype(F32)
    tc = lanes_of(twists[:64], twists[:64])
    ts = lanes_of(twists[64:128], twists[64:128])

    for h in range(2):
        columns = []
        for pair in (2 * h, 2 * h + 1):
            x = lanes_of(xs[pl.ds(2 * pair, 64, stride=8), :], xs[pl.ds(2 * pair + 1, 64, stride=8), :]).astype(BF16)
            a = mm(narrow[:128], rows_of(x, x))
            re, im = a[:64], a[64:]
            b_re = re * tc + im * ts
            b_im = im * tc - re * ts
            columns += [lanes_of(b_re[:, :128], b_im[:, :128]), lanes_of(b_re[:, 128:], b_im[:, 128:])]
        b_high, b_low = halves(rows_of(*columns))
        g = mm_nt(tf_high, b_high) + mm_nt(tf_low, b_high) + mm_nt(tf_high, b_low)
        for n in range(2):
            block = slice(128 * n, 128 * n + 128)
            piece = jnp.where(take_low, g[:256, block], g[256:, block]).astype(BF16)
            sbuf[:, 2 * h + n] = piece.reshape(NF, 16, 128)
    rbuf[pl.ds(f, 1)] = sbuf[pl.ds(f, 1)]

    lane_cap = iota((8, 128), 1)
    gwq[...] = jnp.zeros((5, 8, 128), F32)
    for q in range(4):
        gwq[q, pl.ds(0, CAP), :] = gw[:, 128 * q : 128 * q + 128]
    for n in range(NF):
        shift = fo[n] & 127
        block = fo[n] >> 7
        turn = (128 - shift) & 127
        window = jnp.where(
            lane_cap < 128 - shift, pltpu.roll(gwq[block], turn, 1), pltpu.roll(gwq[block + 1], turn, 1)
        )
        beside = pltpu.roll(pltpu.roll(window, 6, 0), 64, 1)
        wout[n] = jnp.where(lane_cap < 64, window, beside)[:2].astype(BF16)
    wgot[pl.ds(s, 1), pl.ds(f, 1)] = wout[pl.ds(f, 1)][None]

    pl.semaphore_wait(barrier, NF - 1 + s)

    def remote(src, dst, send, recv, to):
        return pltpu.make_async_remote_copy(
            src_ref=src, dst_ref=dst, send_sem=send, recv_sem=recv, device_id=to, device_id_type=MESH
        )

    def everything(buffer, send, recv):
        return remote(buffer, buffer, send, recv, (peers[0], s))

    for p in peers:
        remote(wout.at[p], wgot.at[s, f], sw1, rw1, (p, s)).start()
    for p in peers:
        remote(sbuf.at[p], rbuf.at[f], s1, r1, (p, s)).start()

    def tell(t, carry):
        pl.semaphore_signal(known.at[s], inc=1, device_id=(f, t), device_id_type=MESH)
        return carry

    def hear(t, carry):
        pl.semaphore_wait(known.at[t], 1)
        return carry

    def weights_to(t, carry):
        remote(wgot.at[s], wgot.at[s], sw2, rw2, (f, t)).start()
        return carry

    lax.fori_loop(0, s, tell, 0)

    tback[...] = mm_nt(narrow[128:], picks[...]).astype(BF16)

    lane8 = iota((8, 128), 1)
    left = lane8 < 64
    base = pl.multiple_of(f * MINE, MINE)
    r8 = col[pl.ds(base, MINE), :] & 63
    zero = jnp.zeros((8, 128), F32)
    screen_copy.wait()
    for j in range(MINE):
        shift = so[base + j] & 63
        screen = scr[si[base + j]].astype(F32)
        for part in range(2):
            rolled = [
                pltpu.roll(screen[:, 512 * part + 128 * v : 512 * part + 128 * v + 128], shift, 1) for v in range(4)
            ]
            rolled = [zero] + rolled + [zero]
            for v in range(5):
                piece = jnp.where(lane8 >= shift, rolled[v + 1], rolled[v])
                other = pltpu.roll(piece, 64, 1)
                qsc[part, 2 * v, pl.ds(j, ROWS, stride=MINE), :] = jnp.where(left, piece, other)
                if 2 * v + 1 < BLOCKS:
                    qsc[part, 2 * v + 1, pl.ds(j, ROWS, stride=MINE), :] = jnp.where(left, other, piece)
    for part in range(2):
        for b in range(BLOCKS):
            for pair in range(4):
                at = 16 * pair
                qfin[part, b, :, pl.ds(128 * pair, 128)] = jnp.where(
                    left, qsc[part, b, pl.ds(at, 8), :], qsc[part, b, pl.ds(at + 8, 8), :]
                )

    lane256 = iota((8, 256), 1)
    own = iota((8, 256), 0)
    r8w = lanes_of(r8, r8)
    for n in range(NF):
        first = ((r8w + fo[n]) >> 6) * 16 + own
        for late in range(2):
            spot = first + 16 * late
            at = 256 * late + 16 * n
            spread[pl.ds(at, 16), :] = rows_of(
                jnp.where(lane256 == spot, 1.0, 0.0), jnp.where(lane256 == spot + 8, 1.0, 0.0)
            ).astype(BF16)
        mask = jnp.where((lane8 & 63) >= ((r8 + fo[n]) & 63), 1.0, 0.0)
        low_mask[n] = rows_of(mask, mask).astype(BF16)
    unit = ones_where(iota((SPOTS, 256), 0) == iota((SPOTS, 256), 1))
    gather[...] = mm_nt(unit, spread[...]).astype(BF16)

    everything(wgot.at[0, pl.ds(0, NF - 1)], sw1, rw1).wait_recv()
    lax.fori_loop(0, s, weights_to, 0)

    everything(rbuf.at[pl.ds(0, NF - 1)], s1, r1).wait_recv()

    nothing = jnp.zeros((256 - SPOTS, 256), BF16)
    for h in range(2):
        low, high = [], []
        for pair in (2 * h, 2 * h + 1):
            c = rbuf[:, pair]
            c_low = c * low_mask[...]
            low.append(c_low.reshape(256, 128))
            high.append((c - c_low).reshape(256, 128))
        sums = mm(gather[...], rows_of(lanes_of(*low), lanes_of(*high)))
        done = []
        lanes = pl.ds(256 * h, 256)
        for b in range(BLOCKS):
            re, im = sums[16 * b : 16 * b + 8], sums[16 * b + 8 : 16 * b + 16]
            cs, sn = qfin[0, b, :, lanes], qfin[1, b, :, lanes]
            done += [re * cs - im * sn, re * sn + im * cs]
        both = mm(spread[...], rows_of(rows_of(*done).astype(BF16), nothing))
        keep = low_mask[...].reshape(256, 128) > 0
        for n in range(2):
            block = slice(128 * n, 128 * n + 128)
            piece = jnp.where(keep, both[:256, block], both[256:, block]).astype(BF16)
            esend[h, :, n] = piece.reshape(NF, 16, 128)
        if h == 1:
            for p in peers:
                remote(esend.at[:, p], ebuf.at[:, f], s2, r2, (p, s)).start()
    ebuf[:, pl.ds(f, 1)] = esend[:, pl.ds(f, 1)]

    lax.fori_loop(s + 1, NS, hear, 0)
    lax.fori_loop(s + 1, NS, weights_to, 0)

    ow_row = jnp.broadcast_to(ow_v[...], (128, 128))
    ow_col = jnp.transpose(ow_row)
    earlier = jnp.where((ow_row == ow_col) & (lane < iota((128, 128), 0)), 1.0, 0.0)
    slot = jnp.sum(earlier, axis=1, keepdims=True).astype(jnp.int32)
    weight_row = ow_col * CAP + slot
    spot = 32 * ((weight_row >> 2) & 7) + 2 * (weight_row >> 5) + (weight_row & 1)
    chosen[...] = ones_where(iota((128, 256), 1) == lanes_of(spot, spot))
    upper = (weight_row & 2) == 2
    r_col = (col[...] + fo[f]) & 63
    everything(wgot.at[pl.ds(0, NS - 1)], sw2, rw2).wait_recv()
    rows = mm(chosen[...], wgot[...].reshape(256, 128))
    weight = jnp.where((lane < 64) != upper, rows, pltpu.roll(rows, 64, 1))
    for bit in range(6):
        amount = 1 << bit
        weight = jnp.where((r_col & amount) != 0, pltpu.roll(weight, amount, 1), weight)
    weight4 = both_parts(weight)
    first4 = (lane4 & 63) >= both_parts(r_col)
    wlow[...] = jnp.where(first4, weight4, 0.0).astype(BF16).reshape(NF, 16, 128)
    whigh[...] = jnp.where(first4, 0.0, weight4).astype(BF16).reshape(NF, 16, 128)

    everything(ebuf.at[:, pl.ds(0, NF - 1)], s2, r2).wait_recv()
    for h in range(2):
        low, high = [], []
        for n in range(2):
            e = ebuf[h, :, n]
            low.append((e * wlow[...]).reshape(256, 128))
            high.append((e * whigh[...]).reshape(256, 128))
        d = mm(tback[...], rows_of(lanes_of(*low), lanes_of(*high)))
        d = d[:128] + d[128:]
        re, im = d[:64], d[64:]
        d_re, d_im = [], []
        for turn in range(2):
            at = pl.ds(128 + 64 * turn, 64)
            cs = lanes_of(twists[at, :], twists[at, :])
            at = pl.ds(256 + 64 * turn, 64)
            sn = lanes_of(twists[at, :], twists[at, :])
            d_re.append(re * cs - im * sn)
            d_im.append(re * sn + im * cs)
        d_re, d_im = rows_of(*d_re), rows_of(*d_im)
        d_high, d_low = halves(
            rows_of(lanes_of(d_re[:, :128], d_im[:, :128]), lanes_of(d_re[:, 128:], d_im[:, 128:]))
        )
        o = mm_nt(wide[256:], d_high)
        o = o[:128] + o[128:] + mm_nt(wide[256:384], d_low)
        for n in range(2):
            for r in range(2):
                out[pl.ds(4 * h + 2 * n + r, 64, stride=8), :] = o[64 * r : 64 * r + 64, 128 * n : 128 * n + 128]

    everything(sbuf.at[pl.ds(0, NF - 1)], s1, r1).wait_send()
    everything(wout.at[pl.ds(0, NF - 1)], sw1, rw1).wait_send()
    everything(wgot.at[pl.ds(0, NS - 1)], sw2, rw2).wait_send()
    everything(esend.at[:, pl.ds(0, NF - 1)], s2, r2).wait_send()


def local(strips, facet_offset, subgrid_offset, owner, screen_index, screens, grid_weight):
    twists, narrow, wide = [jnp.asarray(t) for t in make_tables()]
    dma = pltpu.SemaphoreType.DMA
    result = pl.pallas_call(
        kernel,
        out_shape=jax.ShapeDtypeStruct((576, 128), F32),
        in_specs=[pl.BlockSpec(memory_space=pltpu.HBM)] * 11,
        out_specs=pl.BlockSpec(memory_space=pltpu.VMEM),
        scratch_shapes=[
            pltpu.SMEM((16,), jnp.int32),
            pltpu.SMEM((128,), jnp.int32),
            pltpu.SMEM((128,), jnp.int32),
            pltpu.VMEM((1, 128), jnp.int32),
            pltpu.VMEM((1, 128), jnp.int32),
            pltpu.VMEM((ROWS, 2 * FL), BF16),
            pltpu.VMEM((CAP, 512), F32),
            pltpu.VMEM((5, 8, 128), F32),
            pltpu.VMEM((384, 128), F32),
            pltpu.VMEM((384, 128), BF16),
            pltpu.VMEM((512, 256), BF16),
            pltpu.VMEM((16, ROWS, 1024), BF16),
            pltpu.VMEM((576, 128), F32),
            pltpu.VMEM((128, 128), jnp.int32),
            pltpu.VMEM((2, BLOCKS + 1, 128, 128), F32),
            pltpu.VMEM((2, BLOCKS, 8, 512), F32),
            pltpu.VMEM((512, 128), BF16),
            pltpu.VMEM((512, 256), BF16),
            pltpu.VMEM((SPOTS, 512), BF16),
            pltpu.VMEM((NF, 16, 128), BF16),
            pltpu.VMEM((NF, 4, 16, 128), BF16),
            pltpu.VMEM((NF, 4, 16, 128), BF16),
            pltpu.VMEM((2, NF, 2, 16, 128), BF16),
            pltpu.VMEM((2, NF, 2, 16, 128), BF16),
            pltpu.VMEM((NF, 2, 128), BF16),
            pltpu.VMEM((NS, NF, 2, 128), BF16),
            pltpu.VMEM((128, 256), BF16),
            pltpu.VMEM((NF, 16, 128), BF16),
            pltpu.VMEM((NF, 16, 128), BF16),
            pltpu.VMEM((256, 512), BF16),
            dma((10,)), dma, pltpu.SemaphoreType.REGULAR((NS,)), dma, dma, dma, dma, dma, dma, dma, dma,
        ],
        compiler_params=pltpu.CompilerParams(collective_id=0, has_side_effects=True, vmem_limit_bytes=16*1024*1024),
        name="round_trip",
    )(
        *[
            pltpu.with_memory_space_constraint(a, pltpu.HBM)
            for a in (
                facet_offset, subgrid_offset, screen_index, subgrid_offset.reshape(1, -1), owner.reshape(1, -1),
                strips[0], grid_weight, twists, narrow, wide, screens,
            )
        ]
    )
    return result[:512].reshape(64, ROWS, 128).transpose(1, 0, 2).reshape(1, ROWS, 2 * FL)


def solution(mesh):
    in_specs = (P("facet", "sub", None), P(), P(), P(), P(), P(), P(("facet", "sub"), None))
    out_specs = P("facet", "sub", None)
    return jax.shard_map(local, mesh=mesh, in_specs=in_specs, out_specs=out_specs, check_vma=False)
```
